512 devices in a mesh: seq: 32 (over y, x), head: 16 (over z, core).
Axes of the slice: x: 4, y: 8, z: 8, core: 2. Of those that a mesh axis runs over, the one named last changes fastest.
Arguments:
- queries: float32 [32, 8192, 128], P('head', 'seq'), may hold values from -8 to 8
- keys: float32 [32, 8192, 128], P('head', 'seq'), may hold values from -8 to 8
- values: float32 [32, 8192, 128], P('head', 'seq'), may hold values from -6 to 6
- output: float32 [32, 8192, 128], P('head', 'seq'), may hold values from -3 to 3
- grad_output: float32 [32, 8192, 128], P(None, ('seq', 'head')), may hold values from -6 to 6
- mid_offsets: int32 [32, 9], P('head'), may hold values from 0 to 3
- far_offsets: int32 [32], P('head'), may hold values from 0 to 31
- drop_local: int32 [32, 8192, 64], P('head', 'seq'), may hold values from 0 to 4095
- drop_mid: int32 [32, 2048, 64], P('head', 'seq'), may hold values from 0 to 4095
- drop_far: int32 [32, 256, 64], P('head'), may hold values from 0 to 4095
Outputs:
- grad_queries: float32 [32, 8192, 128], P(None, ('seq', 'head'))
- grad_keys: float32 [32, 8192, 128], P(None, ('seq', 'head'))
- grad_values: float32 [32, 8192, 128], P(None, ('seq', 'head'))
The draws below stay inside these ranges and needn't reach their ends.
All inputs are finite; a program needn't handle non-finite values.
Results may differ from the reference program's by a relative error of at most 0.0003.
Values sent between devices are 32-bit elements; how exact they have to be, the bound alone decides.
No kernel may reach another device: no remote copies, remote signals or barrier semaphores. Data moves between devices by JAX's collectives and lax.ppermute only.
A program may use at most 64 MiB of HBM per device.

```python
import jax
import jax.numpy as jnp
from jax import lax

T_DEV = 256
HEAD_DIM = 128
GROUP = 4
TOKENS = 8192
HEADS = 32
SEG_MID = 8
FAR_RATE = 32
N_SEQ = 32


def draw_queries(key, part):
    sampled = jnp.clip(jax.random.normal(jax.random.fold_in(key, 11), (HEADS, TOKENS, HEAD_DIM), jnp.float32), -6.0, 6.0)
    return sampled.astype(jnp.float32)


def draw_keys(key, part):
    sampled = jnp.clip(jax.random.normal(jax.random.fold_in(key, 21), (HEADS, TOKENS, HEAD_DIM), jnp.float32), -6.0, 6.0)
    return sampled.astype(jnp.float32)


def place_ends(result, rng, low, top_value):
    dims = result.shape
    spot = [jax.random.randint(jax.random.fold_in(rng, axis), (), 0, dims[axis]) for axis in range(len(dims))]
    result = result.at[tuple(spot)].set(low)
    longest = dims.index(max(dims))
    spot[longest] = (spot[longest] + 1) % dims[longest]
    return result.at[tuple(spot)].set(top_value)


def shard_levels(stream_key, extent, shards, least, top_value):
    def one(dim, parts):
        heights = jax.random.uniform(jax.random.fold_in(jax.random.fold_in(stream_key, 6), dim), (parts,), jnp.float32, least / len(shards), top_value / len(shards))
        return jnp.repeat(jnp.exp(heights), extent[dim] // parts).reshape((-1,) + (1,) * (len(extent) - dim - 1))

    gain = one(*shards[0])
    for cut in shards[1:]:
        gain = gain * one(*cut)
    return gain


def bell_draw(key, shape, width, bound, pieces=(), kind=jnp.bfloat16):
    values = jax.random.normal(key, shape, jnp.float32) * width
    if len(pieces) > 0:
        values = shard_levels(key, shape, pieces, -0.22, 0.18) * values
    return jnp.clip(values, min=-bound, max=bound).astype(kind)


def setup_inputs(seed: int = 0) -> dict:
    key_of = jax.random.split(jax.random.key(seed), 11)
    queries = draw_queries(jax.random.fold_in(key_of[10], 71), 0)
    keys = draw_keys(jax.random.fold_in(key_of[10], 71), 0)
    values = bell_draw(key_of[2], (HEADS, TOKENS, HEAD_DIM), 1.0, 6.0, ((0, 16), (1, 32)), jnp.float32)
    output = bell_draw(key_of[3], (HEADS, TOKENS, HEAD_DIM), 0.5, 3.0, ((0, 16), (1, 32)), jnp.float32)
    grad_output = bell_draw(key_of[4], (HEADS, TOKENS, HEAD_DIM), 1.0, 6.0, ((1, 512),), jnp.float32)
    mid_offsets = place_ends(jax.random.randint(key_of[5], (HEADS, SEG_MID + 1), 0, GROUP), jax.random.fold_in(key_of[5], 1), 0, GROUP - 1).astype(jnp.int32)
    far_offsets = place_ends(jax.random.randint(key_of[6], (HEADS,), 0, FAR_RATE), jax.random.fold_in(key_of[6], 1), 0, FAR_RATE - 1).astype(jnp.int32)
    drop_local = place_ends(jax.random.randint(key_of[7], (HEADS, TOKENS, T_DEV // 4), 0, 4096), jax.random.fold_in(key_of[7], 1), 0, 4095).astype(jnp.int32)
    drop_mid = place_ends(jax.random.randint(key_of[8], (HEADS, TOKENS // 4, T_DEV // 4), 0, 4096), jax.random.fold_in(key_of[8], 1), 0, 4095).astype(jnp.int32)
    drop_far = place_ends(jax.random.randint(key_of[9], (HEADS, T_DEV, T_DEV // 4), 0, 4096), jax.random.fold_in(key_of[9], 1), 0, 4095).astype(jnp.int32)
    return {"queries": queries, "keys": keys, "values": values, "output": output, "grad_output": grad_output, "mid_offsets": mid_offsets, "far_offsets": far_offsets, "drop_local": drop_local, "drop_mid": drop_mid, "drop_far": drop_far}


keep_level = 7
keep_scale = 8.0 / 7.0
highest = lax.Precision.HIGHEST


def unpack_keep(words):
    bit_starts = jnp.arange(4, dtype=jnp.int32) * 3
    levels = jnp.bitwise_and(jnp.right_shift(words[..., None], bit_starts), 7)
    kept = jnp.where(levels < keep_level, keep_scale, 0.0).astype(jnp.float32)
    return kept.reshape(words.shape[:-1] + (words.shape[-1] * 4,))


def masked_lse(scores, allowed):
    return jax.nn.logsumexp(jnp.where(allowed, scores, -jnp.inf), axis=-1)


def block_grads(scores, allowed, lse_rows, delta_rows, kept, query_rows, key_rows, value_rows, grad_rows, score_scale):
    probs = jnp.where(allowed, jnp.exp(scores - lse_rows[..., None]), 0.0)
    dropped = probs * kept
    grad_probs = jnp.einsum("...qd,...kd->...qk", grad_rows, value_rows, precision=highest) * kept
    grad_scores = probs * (grad_probs - delta_rows[..., None])
    grad_v = jnp.einsum("...qk,...qd->...kd", dropped, grad_rows, precision=highest)
    grad_q = jnp.einsum("...qk,...kd->...qd", grad_scores, key_rows, precision=highest) * score_scale
    grad_k = jnp.einsum("...qk,...qd->...kd", grad_scores, query_rows, precision=highest) * score_scale
    return grad_q, grad_k, grad_v


def one_head(operands):
    queries, keys, values, grad_rows, delta, mid_row, far_start, drop_local, drop_mid, drop_far = operands
    score_scale = HEAD_DIM ** -0.5
    within = jnp.arange(T_DEV, dtype=jnp.int32)
    causal = within[:, None] >= within[None, :]
    local_q = queries.reshape(N_SEQ, T_DEV, HEAD_DIM)
    local_k = keys.reshape(N_SEQ, T_DEV, HEAD_DIM)
    local_v = values.reshape(N_SEQ, T_DEV, HEAD_DIM)
    local_g = grad_rows.reshape(N_SEQ, T_DEV, HEAD_DIM)
    local_scores = jnp.einsum("sqd,skd->sqk", local_q, local_k, precision=highest) * score_scale
    local_lse = masked_lse(local_scores, causal).reshape(TOKENS)
    seg_ids = jnp.arange(SEG_MID + 1, dtype=jnp.int32)
    shift_tokens = (GROUP // 2) * T_DEV
    raw_pos = (seg_ids[:, None] * (GROUP * T_DEV) - shift_tokens + mid_row.astype(jnp.int32)[:, None] + GROUP * within[None, :]).astype(jnp.int32)
    mid_valid = (raw_pos >= 0) & (raw_pos < TOKENS)
    mid_pos = jnp.clip(raw_pos, 0, TOKENS - 1).astype(jnp.int32)
    flat_mid = mid_pos.reshape(-1)
    drop_pos = jnp.where(mid_valid, raw_pos, TOKENS).astype(jnp.int32).reshape(-1)
    mid_allowed = causal[None] & mid_valid[:, :, None] & mid_valid[:, None, :]
    mid_q = queries[mid_pos]
    mid_k = keys[mid_pos]
    mid_v = values[mid_pos]
    mid_g = grad_rows[mid_pos]
    mid_scores = jnp.einsum("sqd,skd->sqk", mid_q, mid_k, precision=highest) * score_scale
    mid_lse = masked_lse(mid_scores, mid_allowed)
    far_pos = (far_start.astype(jnp.int32) + FAR_RATE * within).astype(jnp.int32)
    far_q = queries[far_pos]
    far_k = keys[far_pos]
    far_v = values[far_pos]
    far_g = grad_rows[far_pos]
    far_scores = jnp.einsum("qd,kd->qk", far_q, far_k, precision=highest) * score_scale
    far_lse = masked_lse(far_scores, causal)
    total = local_lse
    total = total.at[drop_pos].set(jnp.logaddexp(total[flat_mid], mid_lse.reshape(-1)), mode="drop")
    total = total.at[far_pos].set(jnp.logaddexp(total[far_pos], far_lse))
    local_keep = unpack_keep(drop_local).reshape(N_SEQ, T_DEV, T_DEV)
    part_q, part_k, part_v = block_grads(local_scores, causal, total.reshape(N_SEQ, T_DEV), delta.reshape(N_SEQ, T_DEV), local_keep, local_q, local_k, local_v, local_g, score_scale)
    grad_q = part_q.reshape(TOKENS, HEAD_DIM)
    grad_k = part_k.reshape(TOKENS, HEAD_DIM)
    grad_v = part_v.reshape(TOKENS, HEAD_DIM)
    keep_rows = jnp.clip(seg_ids[:, None] * T_DEV - (GROUP // 2) * (T_DEV // GROUP) + within[None, :], 0, SEG_MID * T_DEV - 1).astype(jnp.int32)
    mid_keep = unpack_keep(drop_mid)[keep_rows]
    part_q, part_k, part_v = block_grads(mid_scores, mid_allowed, total[mid_pos], delta[mid_pos], mid_keep, mid_q, mid_k, mid_v, mid_g, score_scale)
    grad_q = grad_q.at[drop_pos].add(part_q.reshape(-1, HEAD_DIM), mode="drop")
    grad_k = grad_k.at[drop_pos].add(part_k.reshape(-1, HEAD_DIM), mode="drop")
    grad_v = grad_v.at[drop_pos].add(part_v.reshape(-1, HEAD_DIM), mode="drop")
    far_keep = unpack_keep(drop_far)
    part_q, part_k, part_v = block_grads(far_scores, causal, total[far_pos], delta[far_pos], far_keep, far_q, far_k, far_v, far_g, score_scale)
    grad_q = grad_q.at[far_pos].add(part_q)
    grad_k = grad_k.at[far_pos].add(part_k)
    grad_v = grad_v.at[far_pos].add(part_v)
    return jnp.stack([grad_q, grad_k, grad_v])


def reference(queries, keys, values, output, grad_output, mid_offsets, far_offsets, drop_local, drop_mid, drop_far):
    delta = jnp.sum(grad_output * output, axis=-1)
    stacked = lax.map(one_head, (queries, keys, values, grad_output, delta, mid_offsets, far_offsets, drop_local, drop_mid, drop_far))
    return stacked[:, 0], stacked[:, 1], stacked[:, 2]
```

```python
import functools

import jax
import jax.numpy as jnp
from jax import lax
from jax.experimental import pallas as pl
from jax.experimental.pallas import tpu as pltpu
from jax.sharding import PartitionSpec as P

GROUP = 4
HALF = GROUP // 2
LANES = 128
KEEP_LEVEL = 7
KEEP_SCALE = 8.0 / 7.0
HIGHEST = lax.Precision.HIGHEST
NEG = -1e30


def dot(a, b, dims):
    return lax.dot_general(
        a, b, (dims, ((), ())), precision=HIGHEST, preferred_element_type=jnp.float32
    )


def dot_nt(a, b):
    return dot(a, b, ((1,), (1,)))


def dot_nn(a, b):
    return dot(a, b, ((1,), (0,)))


def dot_tn(a, b):
    return dot(a, b, ((0,), (0,)))


def wide(rows, lanes):
    return rows if lanes == LANES else jnp.concatenate([rows] * (lanes // LANES), axis=1)


def row_max(x):
    return jnp.broadcast_to(jnp.max(x, axis=1, keepdims=True), (x.shape[0], LANES))


def row_sum(x):
    return jnp.broadcast_to(jnp.sum(x, axis=1, keepdims=True), (x.shape[0], LANES))


def log_add(a, b):
    return jnp.maximum(a, b) + jnp.log(1.0 + jnp.exp(-jnp.abs(a - b)))


def masked_lse(scores, allowed):
    masked = jnp.where(allowed, scores, NEG)
    top = row_max(masked)
    return top + jnp.log(row_sum(jnp.exp(masked - wide(top, scores.shape[1]))))


def iotas(rows, cols):
    shape = (rows, cols)
    return lax.broadcasted_iota(jnp.int32, shape, 0), lax.broadcasted_iota(jnp.int32, shape, 1)


def spread_matrix(words):
    source, column = iotas(4 * words, 4 * words)
    chosen = (column % 4 == source // words) & (column // 4 == source % words)
    return jnp.where(chosen, 1.0, 0.0).astype(jnp.bfloat16)


def unpack_keep(words, spread, words_axis):
    kept = [
        jnp.where(((words >> (3 * level)) & 7) < KEEP_LEVEL, 1.0, 0.0) for level in range(4)
    ]
    flags = jnp.concatenate(kept, axis=words_axis).astype(jnp.bfloat16)
    whole = lax.dot_general(
        flags, spread, (((words_axis,), (0,)), ((), ())), preferred_element_type=jnp.float32
    )
    return whole * jnp.float32(KEEP_SCALE)


def pair_terms(scores, allowed, lse, delta, keep, grad_rows, values):
    cols = scores.shape[1]
    probs = jnp.where(allowed, jnp.exp(scores - wide(lse, cols)), 0.0)
    grad_probs = dot_nt(grad_rows, values) * keep
    return probs * keep, probs * (grad_probs - wide(delta, cols))


def place_info():
    place = lax.axis_index("seq")
    shifted = place + HALF
    return place, shifted // GROUP, shifted % GROUP


def prep_kernel(mid_off, far_off, k_ref, v_ref, mid_out, far_out):
    _, segment, _ = place_info()
    heads, rows, _ = k_ref.shape
    count = far_out.shape[0]
    far_rows = rows // count
    for head in range(heads):
        mid = mid_off[head, segment]
        far = far_off[head]
        for side, ref in enumerate((k_ref, v_ref)):
            mid_out[side, head] = ref[head, pl.ds(mid, rows // GROUP, stride=GROUP), :]
            picked = ref[head, pl.ds(far, far_rows, stride=count), :]
            for dest in range(count):
                far_out[dest, side * heads + head] = picked


def local_kernel(q_ref, k_ref, words_ref, scores_out, lse_out, keep_out, keep_buf):
    place, _, _ = place_info()
    heads, rows, width = q_ref.shape
    far_rows = keep_out.shape[1]
    spread = spread_matrix(words_ref.shape[1])
    row, col = iotas(rows, rows)
    for head in range(heads):
        scores = dot_nt(q_ref[head], k_ref[head]) * (width**-0.5)
        scores_out[head] = scores
        lse_out[head] = masked_lse(scores, row >= col)
        keep_buf[...] = unpack_keep(words_ref[head], spread, 0)
        keep_out[head] = keep_buf[pl.ds(place * far_rows, far_rows), :]


def mid_allowed(place, pos, quarter, cols):
    row, col = iotas(quarter, cols)
    return (col <= pos * quarter + row) & (place - pos + col // quarter >= 0)


def mid_kernel(
    mid_off, q_ref, g_ref, o_ref, lse_ref, kv0, kv1, kv2, kv3,
    g_out, delta_out, lse_out, scores_out, kv_out,
):
    place, segment, pos = place_info()
    heads, rows, width = q_ref.shape
    quarter = rows // GROUP
    for distance, ref in enumerate((kv0, kv1, kv2, kv3)):
        start = ((pos - distance) % GROUP) * quarter
        for side in range(2):
            for head in range(heads):
                kv_out[side, head, pl.ds(start, quarter), :] = ref[side, head]
    allowed = mid_allowed(place, pos, quarter, rows)
    for head in range(heads):
        g = g_ref[:, head].reshape(rows, width)
        g_out[head] = g
        delta_out[head] = row_sum(g * o_ref[head])
        picked = pl.ds(mid_off[head, segment], quarter, stride=GROUP)
        scores = dot_nt(q_ref[head, picked, :], kv_out[0, head]) * (width**-0.5)
        scores_out[head] = scores
        lse_out[head] = lse_ref[head]
        lse_out[head, picked, :] = log_add(lse_ref[head, picked, :], masked_lse(scores, allowed))


def far_kernel(
    far_off, q_ref, g_ref, delta_ref, lse_ref, keep_ref, kv_ref,
    lse_out, back_out, gq_out,
):
    place, _, _ = place_info()
    heads, rows, width = q_ref.shape
    count = kv_ref.shape[0]
    far_rows = rows // count
    scale = width**-0.5
    row, col = iotas(far_rows, rows)
    allowed = col <= place * far_rows + row
    for head in range(heads):
        picked = pl.ds(far_off[head], far_rows, stride=count)
        far_q = q_ref[head, picked, :]
        far_g = g_ref[head, picked, :]
        far_k = kv_ref[:, head].reshape(rows, width)
        far_v = kv_ref[:, heads + head].reshape(rows, width)
        scores = dot_nt(far_q, far_k) * scale
        lse = log_add(lse_ref[head, picked, :], masked_lse(scores, allowed))
        lse_out[head] = lse_ref[head]
        lse_out[head, picked, :] = lse
        dropped, grad_scores = pair_terms(
            scores, allowed, lse, delta_ref[head, picked, :], keep_ref[head], far_g, far_v
        )
        gq_out[head] = dot_nn(grad_scores, far_k) * scale
        gk = dot_tn(grad_scores, far_q) * scale
        gv = dot_tn(dropped, far_g)
        back_out[:, head] = gk.reshape(count, far_rows, width)
        back_out[:, heads + head] = gv.reshape(count, far_rows, width)


def mid_grad_kernel(
    mid_off, q_ref, g_ref, delta_ref, lse_ref, words_ref, scores_ref, kv_ref,
    gq_out, own_out, out1, out2, out3, gk_buf, gv_buf,
):
    place, segment, pos = place_info()
    heads, rows, width = q_ref.shape
    quarter = rows // GROUP
    scale = width**-0.5
    spread = spread_matrix(words_ref.shape[2])
    allowed = mid_allowed(place, pos, quarter, rows)
    for head in range(heads):
        picked = pl.ds(mid_off[head, segment], quarter, stride=GROUP)
        mid_q = q_ref[head, picked, :]
        mid_g = g_ref[head, picked, :]
        keep = unpack_keep(words_ref[head], spread, 1)
        dropped, grad_scores = pair_terms(
            scores_ref[head], allowed, lse_ref[head, picked, :], delta_ref[head, picked, :],
            keep, mid_g, kv_ref[1, head],
        )
        gq_out[head] = dot_nn(grad_scores, kv_ref[0, head]) * scale
        gk_buf[...] = dot_tn(grad_scores, mid_q) * scale
        gv_buf[...] = dot_tn(dropped, mid_g)
        for distance, ref in enumerate((own_out, out1, out2, out3)):
            block = pl.ds(((pos - distance) % GROUP) * quarter, quarter)
            ref[0, head] = gk_buf[block, :]
            ref[1, head] = gv_buf[block, :]


def local_grad_kernel(
    mid_off, far_off, q_ref, k_ref, v_ref, g_ref, delta_ref, lse_ref, words_ref, scores_ref,
    mid_gq, far_gq, gq_out, gk_out, gv_out,
):
    _, segment, _ = place_info()
    heads, rows, width = q_ref.shape
    quarter = rows // GROUP
    far_rows = far_gq.shape[1]
    scale = width**-0.5
    spread = spread_matrix(words_ref.shape[1])
    row, col = iotas(rows, rows)
    allowed = row >= col
    for head in range(heads):
        keep = unpack_keep(words_ref[head], spread, 0)
        dropped, grad_scores = pair_terms(
            scores_ref[head], allowed, lse_ref[head], delta_ref[head], keep,
            g_ref[head], v_ref[head],
        )
        gq_out[head] = dot_nn(grad_scores, k_ref[head]) * scale
        gk_out[head] = dot_tn(grad_scores, q_ref[head]) * scale
        gv_out[head] = dot_tn(dropped, g_ref[head])
        mid = pl.ds(mid_off[head, segment], quarter, stride=GROUP)
        far = pl.ds(far_off[head], far_rows, stride=rows // far_rows)
        gq_out[head, mid, :] = gq_out[head, mid, :] + mid_gq[head]
        gq_out[head, far, :] = gq_out[head, far, :] + far_gq[head]


def final_kernel(
    mid_off, far_off, gq_ref, gk_ref, gv_ref, own_ref, back1, back2, back3, far_ref,
    out, gk_buf, gv_buf,
):
    _, segment, _ = place_info()
    heads, rows, width = gq_ref.shape
    quarter = rows // GROUP
    count = far_ref.shape[0]
    far_rows = rows // count
    parts = out.shape[0]
    far_sum = jnp.sum(far_ref[...], axis=0)
    for head in range(heads):
        mid = pl.ds(mid_off[head, segment], quarter, stride=GROUP)
        far = pl.ds(far_off[head], far_rows, stride=count)
        out[:, 0, head] = gq_ref[head].reshape(parts, rows // parts, width)
        for side, (ref, buf) in enumerate(((gk_ref, gk_buf), (gv_ref, gv_buf))):
            buf[...] = ref[head]
            returned = own_ref[side, head] + back1[side, head] + back2[side, head] + back3[side, head]
            buf[mid, :] = buf[mid, :] + returned
            buf[far, :] = buf[far, :] + far_sum[side * heads + head]
            out[:, 1 + side, head] = buf[...].reshape(parts, rows // parts, width)


def call(kernel, scalars, arrays, outs, scratch=(), flops=0):
    smem = [pl.BlockSpec(memory_space=pltpu.SMEM)] * len(scalars)
    vmem = [pl.BlockSpec(memory_space=pltpu.VMEM)] * len(arrays)
    shapes = [jax.ShapeDtypeStruct(shape, jnp.float32) for shape in outs]
    moved = 4 * sum(a.size for a in arrays) + 4 * sum(s.size for s in shapes)
    result = pl.pallas_call(
        kernel,
        out_shape=shapes,
        in_specs=smem + vmem,
        out_specs=[pl.BlockSpec(memory_space=pltpu.VMEM)] * len(outs),
        scratch_shapes=[pltpu.VMEM(shape, jnp.float32) for shape in scratch],
        cost_estimate=pl.CostEstimate(flops=flops, transcendentals=0, bytes_accessed=moved),
        compiler_params=pltpu.CompilerParams(vmem_limit_bytes=40 * 1024 * 1024),
    )(*scalars, *arrays)
    return result


def shifted(value, steps):
    count = lax.axis_size("seq")
    first, last = max(0, -steps), min(count, count - steps)
    return lax.ppermute(value, "seq", [(source, source + steps) for source in range(first, last)])


def exchange(value, axis):
    return lax.all_to_all(value, axis, split_axis=0, concat_axis=0, tiled=True)


def per_device(q, k, v, output, grad_output, mid_off, far_off, drop_local, drop_mid, drop_far):
    heads, rows, width = q.shape
    count = lax.axis_size("seq")
    parts = lax.axis_size("head")
    quarter = rows // GROUP
    far_rows = rows // count
    whole = (heads, rows, width)
    pairs = (heads, rows, rows)
    mid_kv = (2, heads, quarter, width)
    far_kv = (count, 2 * heads, far_rows, width)
    block = 6 * 2 * heads * rows * rows * width

    g_parts = exchange(grad_output.reshape(parts, heads, rows // parts, width), "head")
    own_kv, far_send = call(prep_kernel, (mid_off, far_off), (k, v), (mid_kv, far_kv))
    received = [shifted(own_kv, distance) for distance in range(1, GROUP)]
    far_received = exchange(far_send, "seq")
    drop_local = jnp.swapaxes(drop_local, 1, 2)
    drop_far = jnp.swapaxes(drop_far, 1, 2)
    scores, lse, far_keep = call(
        local_kernel,
        (),
        (q, k, drop_far),
        (pairs, whole, (heads, far_rows, rows)),
        scratch=((rows, rows),),
        flops=block,
    )
    g, delta, lse, mid_scores, mid_kv_all = call(
        mid_kernel,
        (mid_off,),
        (q, g_parts, output, lse, own_kv, *received),
        (whole, whole, whole, (heads, quarter, rows), (2, heads, rows, width)),
        flops=block // GROUP,
    )
    lse, far_back, far_gq = call(
        far_kernel,
        (far_off,),
        (q, g, delta, lse, far_keep, far_received),
        (whole, far_kv, (heads, far_rows, width)),
        flops=block // GROUP,
    )
    far_returned = exchange(far_back, "seq")
    mid_gq, mid_own, *outgoing = call(
        mid_grad_kernel,
        (mid_off,),
        (q, g, delta, lse, drop_mid, mid_scores, mid_kv_all),
        ((heads, quarter, width), mid_kv, mid_kv, mid_kv, mid_kv),
        scratch=((rows, width), (rows, width)),
        flops=block,
    )
    returned = [shifted(value, -distance - 1) for distance, value in enumerate(outgoing)]
    gq, gk, gv = call(
        local_grad_kernel,
        (mid_off, far_off),
        (q, k, v, g, delta, lse, drop_local, scores, mid_gq, far_gq),
        (whole, whole, whole),
        flops=4 * block,
    )
    (stacked,) = call(
        final_kernel,
        (mid_off, far_off),
        (gq, gk, gv, mid_own, *returned, far_returned),
        ((parts, 3, heads, rows // parts, width),),
        scratch=((rows, width), (rows, width)),
    )
    result = exchange(stacked, "head")
    shape = (parts * heads, rows // parts, width)
    return tuple(result[:, part].reshape(shape) for part in range(3))


def solution(mesh):
    tokens = P(None, ("seq", "head"), None)
    placed = P("head", "seq", None)
    return jax.shard_map(
        per_device,
        mesh=mesh,
        in_specs=(
            placed, placed, placed, placed, tokens,
            P("head", None), P("head"), placed, placed, P("head", None, None),
        ),
        out_specs=(tokens, tokens, tokens),
        check_vma=False,
    )
```

```python
import math

import jax
import jax.numpy as jnp
from jax import lax
from jax.experimental import pallas as pl
from jax.experimental.pallas import tpu as pltpu
from jax.sharding import PartitionSpec as P

GROUP = 4
HALF = GROUP // 2
LANES = 128
ACROSS = 4
KEEP_LEVEL = 7
KEEP_SCALE = 8.0 / 7.0
HIGHEST = lax.Precision.HIGHEST
NEG = -1e30


def dot(a, b, dims):
    return lax.dot_general(
        a, b, (dims, ((), ())), precision=HIGHEST, preferred_element_type=jnp.float32
    )


def dot_nt(a, b):
    return dot(a, b, ((1,), (1,)))


def dot_nn(a, b):
    return dot(a, b, ((1,), (0,)))


def dot_tn(a, b):
    return dot(a, b, ((0,), (0,)))


def wide(rows, lanes):
    if lanes <= LANES:
        return rows[:, :lanes]
    return jnp.concatenate([rows] * (lanes // LANES), axis=1)


def row_max(x):
    return jnp.broadcast_to(jnp.max(x, axis=1, keepdims=True), (x.shape[0], LANES))


def row_sum(x):
    return jnp.broadcast_to(jnp.sum(x, axis=1, keepdims=True), (x.shape[0], LANES))


def log_add(a, b):
    return jnp.maximum(a, b) + jnp.log(1.0 + jnp.exp(-jnp.abs(a - b)))


def masked_lse(scores, allowed):
    masked = jnp.where(allowed, scores, NEG)
    top = row_max(masked)
    return top + jnp.log(row_sum(jnp.exp(masked - wide(top, scores.shape[1]))))


def iotas(rows, cols):
    shape = (rows, cols)
    return lax.broadcasted_iota(jnp.int32, shape, 0), lax.broadcasted_iota(jnp.int32, shape, 1)


def spread_matrix(words, first, cols):
    source, column = iotas(4 * words, cols)
    column = column + first
    chosen = (column % 4 == source // words) & (column // 4 == source % words)
    return jnp.where(chosen, 1.0, 0.0).astype(jnp.bfloat16)


def keep_flags(words, axis):
    kept = [
        jnp.where(((words >> (3 * level)) & 7) < KEEP_LEVEL, 1.0, 0.0) for level in range(4)
    ]
    return jnp.concatenate(kept, axis=axis).astype(jnp.bfloat16)


def spread_flags(flags, spread, axis):
    whole = lax.dot_general(
        flags, spread, (((axis,), (0,)), ((), ())), preferred_element_type=jnp.float32
    )
    return whole * jnp.float32(KEEP_SCALE)


def pair_terms(scores, allowed, lse, delta, keep, grad_rows, values):
    cols = scores.shape[1]
    probs = jnp.where(allowed, jnp.exp(scores - wide(lse, cols)), 0.0)
    grad_probs = dot_nt(grad_rows, values) * keep
    return probs * keep, probs * (grad_probs - wide(delta, cols))


def place_info():
    place = lax.axis_index("seq")
    shifted = place + HALF
    return place, shifted // GROUP, shifted % GROUP


def place_masks(place, pos, quarter, rows):
    row, col = iotas(quarter, rows)
    return (col <= pos * quarter + row) & (place - pos + col // quarter >= 0)


def prep_kernel(mid_off, x, o):
    _, segment, _ = place_info()
    heads, rows, _ = x.k.shape
    for head in range(heads):
        picked = pl.ds(mid_off[head, segment], rows // GROUP, stride=GROUP)
        o.own_kv[0, head] = x.k[head, picked, :]
        o.own_kv[1, head] = x.v[head, picked, :]


def local_kernel(mid_off, far_off, x, o):
    heads, rows, width = x.q.shape
    row, col = iotas(rows, rows)
    for head in range(heads):
        o.lse[head] = masked_lse(dot_nt(x.q[head], x.k[head]) * (width**-0.5), row >= col)


def gather_mid(x, side, head, buf):
    _, _, pos = place_info()
    quarter = x.kv0.shape[2]
    for distance in range(GROUP):
        start = ((pos - distance) % GROUP) * quarter
        buf[pl.ds(start, quarter), :] = x[f"kv{distance}"][side, head]


def mid_kernel(mid_off, far_off, x, o, buf):
    place, segment, pos = place_info()
    heads, rows, width = x.q.shape
    quarter = rows // GROUP
    count, sends = lax.axis_size("seq"), o.far_send.shape[0]
    far_rows = rows // count
    line = place // (count // sends)
    for head in range(heads):
        o.g[head] = x.g_parts[:, head].reshape(rows, width)
        far = pl.ds(far_off[head], far_rows, stride=count)
        far_q, far_k, far_v = x.q[head, far, :], x.k[head, far, :], x.v[head, far, :]
        far_g = o.g[head, far, :]
        for dest in range(sends):
            o.far_send[dest, head] = far_k
            o.far_send[dest, heads + head] = jnp.where(dest >= line, far_v, far_q)
            o.far_send[dest, 2 * heads + head] = far_g
    allowed = place_masks(place, pos, quarter, rows)
    _, lane = iotas(far_rows, LANES)
    part = lane // (LANES // (2 * heads))
    row_facts = jnp.zeros((far_rows, LANES), jnp.float32)
    for head in range(heads):
        o.delta[head] = row_sum(o.g[head] * x.output[head])
        gather_mid(x, 0, head, buf)
        mid = pl.ds(mid_off[head, segment], quarter, stride=GROUP)
        far = pl.ds(far_off[head], far_rows, stride=count)
        scores = dot_nt(x.q[head, mid, :], buf[...]) * (width**-0.5)
        o.lse[head] = x.lse[head]
        o.lse[head, mid, :] = log_add(x.lse[head, mid, :], masked_lse(scores, allowed))
        row_facts = jnp.where(part == 2 * head, o.lse[head, far, :], row_facts)
        row_facts = jnp.where(part == 2 * head + 1, o.delta[head, far, :], row_facts)
    for dest in range(sends):
        o.far_send[dest, 3 * heads] = row_facts


def relay_kernel(mid_off, far_off, x, o):
    place, _, _ = place_info()
    heads, rows, _ = x.q.shape
    sends = o.relay.shape[0]
    lines = x.column.shape[0]
    for dest in range(sends):
        o.relay[dest] = x.column[...]
    for head in range(heads):
        far_q = x.q[head, pl.ds(far_off[head], rows // (lines * sends), stride=lines * sends), :]
        far_v = x.column[place // sends, heads + head]
        for dest in range(sends):
            o.relay[dest, place // sends, heads + head] = jnp.where(
                dest >= place % sends, far_v, far_q
            )


def rows_kernel(mid_off, far_off, x, o):
    _, segment, _ = place_info()
    heads, rows, width = x.q.shape
    quarter = rows // GROUP
    words = x.drop_mid.shape[2]
    _, lane = iotas(quarter, LANES)
    for head in range(heads):
        mid = pl.ds(mid_off[head, segment], quarter, stride=GROUP)
        o.rows[0, head] = x.q[head, mid, :]
        o.rows[1, head] = x.g[head, mid, :]
        o.rows[2, head] = jnp.where(
            lane < words + (LANES - words) // 2, x.lse[head, mid, :], x.delta[head, mid, :]
        )
        o.rows[2, head, :, 0:words] = x.drop_mid[head].astype(jnp.float32)


def terms_kernel(mid_off, far_off, x, o, buf, keep_buf):
    place, segment, _ = place_info()
    heads, rows, width = x.q.shape
    scale = width**-0.5
    words = x.drop_local.shape[1]
    far_rows = o.far_keep.shape[1]
    spread = spread_matrix(words, 0, rows)
    far_spread = spread_matrix(words, place * far_rows, far_rows)
    for head in range(heads):
        o.scores[head] = dot_nt(x.q[head], x.k[head]) * scale
        keep = spread_flags(keep_flags(x.drop_local[head], 0), spread, 0)
        o.keep[head] = keep
        o.terms[head] = dot_nt(x.g[head], x.v[head]) * keep - wide(x.delta[head], rows)
        mid = pl.ds(mid_off[head, segment], rows // GROUP, stride=GROUP)
        gather_mid(x, 0, head, buf)
        o.mid_k[head] = buf[...]
        o.mid_scores[head] = dot_nt(x.q[head, mid, :], buf[...]) * scale
        gather_mid(x, 1, head, buf)
        keep = spread_flags(keep_flags(x.drop_mid[head], 1), spread, 1)
        o.mid_terms[head] = dot_nt(x.g[head, mid, :], buf[...]) * keep - wide(
            x.delta[head, mid, :], rows
        )
        flags = keep_flags(x.drop_far[head], 0)
        keep_buf[...] = spread_flags(flags, spread, 0)
        o.far_keep[head] = keep_buf[pl.ds(place * far_rows, far_rows), :]
        o.far_cols[:, head * far_rows : (head + 1) * far_rows] = spread_flags(flags, far_spread, 0)


def fact(facts, index, share):
    return jnp.broadcast_to(facts[:, index * share : index * share + 1], facts.shape)


def grad_kernel(
    mid_off, far_off, x, o, q_buf, lse_buf, far_lse, key_lse, gq_buf, gk_buf, gv_buf, score_buf,
    far_ref,
):
    place, segment, pos = place_info()
    heads, rows, width = x.q.shape
    quarter = rows // GROUP
    parts = o.stacked.shape[0]
    count = far_ref.shape[0]
    across, lines = x.far.shape[:2]
    for source in range(count):
        far_ref[source] = x.far[source % across, source // across]
    far_rows = rows // count
    scale = width**-0.5
    share = LANES // (2 * heads)
    words = quarter
    row, col = iotas(rows, rows)
    causal = row >= col
    far_row, far_col = iotas(far_rows, rows)
    far_allowed = far_col <= place * far_rows + far_row
    key_row, key_col = iotas(rows, far_rows)
    far_key_allowed = place * far_rows + key_col <= key_row
    mid_allowed = place_masks(place, pos, quarter, rows)
    mid_row, mid_col = iotas(rows, quarter)
    distance = mid_row // quarter
    later = (distance > 0) & (pos + distance < GROUP) & (place + distance < count)
    mid_key_allowed = later | ((distance == 0) & (mid_row >= mid_col))
    facts = far_ref[:, 3 * heads].reshape(rows, LANES)
    own = pl.ds(place * far_rows, far_rows)
    spread = spread_matrix(words, pos * quarter, quarter)
    for head in range(heads):
        mid_start = mid_off[head, segment]
        mid = pl.ds(mid_start, quarter, stride=GROUP)
        far = pl.ds(far_off[head], far_rows, stride=count)
        all_k = far_ref[:, head].reshape(rows, width)
        all_v = far_ref[:, heads + head].reshape(rows, width)
        all_g = far_ref[:, 2 * heads + head].reshape(rows, width)
        far_q = x.q[head, far, :]
        q_buf[...] = all_v
        q_buf[own, :] = far_q
        all_q = q_buf[...]
        score_buf[...] = dot_nt(all_q, all_k) * scale
        far_lse[...] = log_add(fact(facts, 2 * head, share), masked_lse(score_buf[...], causal))
        lse_buf[...] = x.lse[head]
        lse_buf[far, :] = far_lse[own, :]

        probs = jnp.where(causal, jnp.exp(x.scores[head] - wide(lse_buf[...], rows)), 0.0)
        grad_scores = probs * x.terms[head]
        gq_buf[...] = dot_nn(grad_scores, x.k[head]) * scale
        gk_buf[...] = dot_tn(grad_scores, x.q[head]) * scale
        gv_buf[...] = dot_tn(probs * x.keep[head], x.g[head])

        probs = jnp.where(
            mid_allowed, jnp.exp(x.mid_scores[head] - wide(lse_buf[mid, :], rows)), 0.0
        )
        grad_scores = probs * x.mid_terms[head]
        gq_buf[mid, :] = gq_buf[mid, :] + dot_nn(grad_scores, x.mid_k[head]) * scale

        dropped, grad_scores = pair_terms(
            score_buf[own, :], far_allowed, lse_buf[far, :],
            fact(far_ref[place, 3 * heads], 2 * head + 1, share),
            x.far_keep[head], far_ref[place, 2 * heads + head], all_v,
        )
        gq_buf[far, :] = gq_buf[far, :] + dot_nn(grad_scores, all_k) * scale
        o.stacked[:, 0, head] = gq_buf[...].reshape(parts, rows // parts, width)

        key_lse[0:quarter, :] = lse_buf[mid, :]
        meets = far_off[head] % GROUP == mid_start
        first = jnp.where(meets, (far_off[head] - mid_start) // GROUP, 0)
        for step in range(1, GROUP):
            key_lse[step * quarter : (step + 1) * quarter, :] = jnp.broadcast_to(
                x[f"rows{step}"][2, head][:, words : words + 1], (quarter, LANES)
            )
            spots = pl.ds(step * quarter + first, far_rows, stride=count // GROUP)
            source = jnp.minimum(place + step, count - 1) * far_rows
            key_lse[spots, :] = jnp.where(
                meets, far_lse[pl.ds(source, far_rows), :], key_lse[spots, :]
            )
        mid_q = jnp.concatenate([x[f"rows{step}"][0, head] for step in range(GROUP)], axis=0)
        mid_g = jnp.concatenate([x[f"rows{step}"][1, head] for step in range(GROUP)], axis=0)
        mid_facts = jnp.concatenate([x[f"rows{step}"][2, head] for step in range(GROUP)], axis=0)
        keep = spread_flags(keep_flags(mid_facts[:, 0:words].astype(jnp.int32), 1), spread, 1)
        dropped, grad_scores = pair_terms(
            dot_nt(mid_q, x.own_kv[0, head]) * scale, mid_key_allowed, key_lse[...],
            jnp.broadcast_to(mid_facts[:, LANES - 1 : LANES], (rows, LANES)),
            keep, mid_g, x.own_kv[1, head],
        )
        gk_buf[mid, :] = gk_buf[mid, :] + dot_tn(grad_scores, mid_q) * scale
        gv_buf[mid, :] = gv_buf[mid, :] + dot_tn(dropped, mid_g)

        far_k, far_v = far_ref[place, head], far_ref[place, heads + head]
        dropped, grad_scores = pair_terms(
            dot_nt(all_q, far_k) * scale, far_key_allowed, far_lse[...],
            fact(facts, 2 * head + 1, share),
            x.far_cols[:, head * far_rows : (head + 1) * far_rows], all_g, far_v,
        )
        gk_buf[far, :] = gk_buf[far, :] + dot_tn(grad_scores, all_q) * scale
        gv_buf[far, :] = gv_buf[far, :] + dot_tn(dropped, all_g)
        o.stacked[:, 1, head] = gk_buf[...].reshape(parts, rows // parts, width)
        o.stacked[:, 2, head] = gv_buf[...].reshape(parts, rows // parts, width)


class Loaded:
    def __init__(self, direct, fetched):
        self.__dict__.update(direct=direct, fetched=fetched, seen=set())

    def __getitem__(self, name):
        if name in self.direct:
            return self.direct[name]
        copy, ref = self.fetched[name]
        if name not in self.seen:
            self.seen.add(name)
            copy.wait()
        return ref

    def __getattr__(self, name):
        return self[name]


class Stored:
    def __init__(self, refs, sends):
        self.__dict__.update(refs, sends=sends)

    def send(self, name, part=slice(None)):
        self.sends(name, part)


def call(kernel, scalars, arrays, outs, scratch=(), flops=0, fetched=()):
    names = list(arrays)
    loads = [name for name in names if name in fetched]
    out_names = [name.rstrip("+") for name in outs]
    shapes = dict(zip(out_names, outs.values()))
    saves = [name for name in outs if not name.endswith("+")]
    hbm, vmem = pl.BlockSpec(memory_space=pltpu.HBM), pl.BlockSpec(memory_space=pltpu.VMEM)

    def run(*refs):
        refs = list(refs)

        def take(count):
            taken, refs[:] = refs[:count], refs[count:]
            return taken

        scalar_refs, in_refs, out_refs = take(len(scalars)), take(len(names)), take(len(outs))
        in_bufs, out_bufs, extra = take(len(loads)), take(len(saves)), take(len(scratch))
        in_sems, out_sems = refs
        given, written = dict(zip(names, in_refs)), dict(zip(out_names, out_refs))
        copies = {
            name: (pltpu.make_async_copy(given[name], buf, in_sems.at[i]), buf)
            for i, (name, buf) in enumerate(zip(loads, in_bufs))
        }
        for copy, _ in copies.values():
            copy.start()
        loaded = Loaded({name: given[name] for name in names if name not in loads}, copies)
        buffers = dict(zip(saves, out_bufs))
        writes = []

        def send(name, part=slice(None)):
            write = pltpu.make_async_copy(
                buffers[name].at[part], written[name].at[part], out_sems.at[len(writes)]
            )
            write.start()
            writes.append(write)
            sent.add(name)

        sent = set()
        kernel(*scalar_refs, loaded, Stored({**written, **buffers}, send), *extra)
        for name in loads:
            loaded[name]
        for name in saves:
            if name not in sent:
                send(name)
        for write in writes:
            write.wait()

    values = list(arrays.values())
    moved = 4 * sum(math.prod(shape) for shape in [v.shape for v in values] + [*shapes.values()])
    result = pl.pallas_call(
        run,
        out_shape=[
            pltpu.HBM(shape, jnp.float32)
            if name in saves
            else jax.ShapeDtypeStruct(shape, jnp.float32)
            for name, shape in shapes.items()
        ],
        in_specs=[pl.BlockSpec(memory_space=pltpu.SMEM)] * len(scalars)
        + [hbm if name in loads else vmem for name in names],
        out_specs=[hbm if name in saves else vmem for name in shapes],
        scratch_shapes=[pltpu.VMEM(arrays[name].shape, arrays[name].dtype) for name in loads]
        + [pltpu.VMEM(shapes[name], jnp.float32) for name in saves]
        + [pltpu.VMEM(shape, jnp.float32) for shape in scratch]
        + [
            pltpu.SemaphoreType.DMA((max(len(loads), 1),)),
            pltpu.SemaphoreType.DMA((max(2 * len(saves), 1),)),
        ],
        cost_estimate=pl.CostEstimate(flops=flops, transcendentals=0, bytes_accessed=moved),
        compiler_params=pltpu.CompilerParams(vmem_limit_bytes=40 * 1024 * 1024),
    )(
        *scalars,
        *[
            pltpu.with_memory_space_constraint(value, pltpu.HBM) if name in loads else value
            for name, value in arrays.items()
        ],
    )
    return dict(zip(out_names, result))


def shifted(value, steps):
    count = lax.axis_size("seq")
    first, last = max(0, -steps), min(count, count - steps)
    return lax.ppermute(value, "seq", [(source, source + steps) for source in range(first, last)])


def exchange(value, axis, groups=None):
    return lax.all_to_all(
        value, axis, split_axis=0, concat_axis=0, tiled=True, axis_index_groups=groups
    )


def per_device(q, k, v, output, grad_output, mid_off, far_off, drop_local, drop_mid, drop_far):
    heads, rows, width = q.shape
    count = lax.axis_size("seq")
    parts = lax.axis_size("head")
    quarter = rows // GROUP
    far_rows = rows // count
    whole = (heads, rows, width)
    pairs = (heads, rows, rows)
    mid_pairs = (heads, quarter, rows)
    key_pairs = (heads, rows, quarter)
    block = 6 * 2 * heads * rows * rows * width
    drop_local = jnp.swapaxes(drop_local, 1, 2)
    drop_far = jnp.swapaxes(drop_far, 1, 2)
    offsets = (mid_off, far_off)
    lines = count // ACROSS
    rows_of = [[line * ACROSS + i for i in range(ACROSS)] for line in range(lines)]
    columns = [list(group) for group in zip(*rows_of)]

    g_parts = exchange(grad_output.reshape(parts, heads, rows // parts, width), "head")
    own_kv = call(
        prep_kernel, (mid_off,), {"k": k, "v": v}, {"own_kv+": (2, heads, quarter, width)}
    )["own_kv"]
    kv = {f"kv{step}": shifted(own_kv, step) if step else own_kv for step in range(GROUP)}
    lse = call(local_kernel, offsets, {"q": q, "k": k}, {"lse+": whole}, flops=block)["lse"]
    mid = call(
        mid_kernel,
        offsets,
        {"g_parts": g_parts, "q": q, "k": k, "v": v, **kv, "output": output, "lse": lse},
        {
            "g+": whole,
            "delta+": whole,
            "lse+": whole,
            "far_send+": (lines, 3 * heads + 1, far_rows, width),
        },
        scratch=((rows, width),),
        flops=block // GROUP,
    )
    column = exchange(mid.pop("far_send"), "seq", columns)
    own_rows = call(
        rows_kernel, offsets, {"q": q, **mid, "drop_mid": drop_mid},
        {"rows+": (3, heads, quarter, width)},
    )["rows"]
    mid_rows = {
        f"rows{step}": shifted(own_rows, -step) if step else own_rows for step in range(GROUP)
    }
    relay = call(
        relay_kernel,
        offsets,
        {"column": column, "q": q},
        {"relay+": (ACROSS, lines, 3 * heads + 1, far_rows, width)},
    )["relay"]
    far = exchange(relay, "seq", rows_of)
    terms = call(
        terms_kernel,
        offsets,
        {
            "q": q, "k": k, "v": v, "g": mid["g"], "delta": mid["delta"], **kv,
            "drop_local": drop_local, "drop_mid": drop_mid, "drop_far": drop_far,
        },
        {
            "scores": pairs,
            "keep": pairs,
            "terms": pairs,
            "mid_scores": mid_pairs,
            "mid_terms": mid_pairs,
            "mid_k": whole,
            "far_keep": (heads, far_rows, rows),
            "far_cols": (rows, heads * far_rows),
        },
        scratch=((rows, width), (rows, rows)),
        flops=2 * block,
    )
    stacked = call(
        grad_kernel,
        offsets,
        {
            "far": far, "q": q, "k": k, "g": mid["g"], "lse": mid["lse"],
            **terms, **mid_rows, "own_kv": own_kv,
        },
        {"stacked+": (parts, 3, heads, rows // parts, width)},
        scratch=((rows, width),) * 7
        + ((rows, rows), (count, 3 * heads + 1, far_rows, width)),
        flops=8 * block,
        fetched=("k", "rows1", "rows2", "rows3", *terms),
    )["stacked"]
    result = exchange(stacked, "head")
    shape = (parts * heads, rows // parts, width)
    return tuple(result[:, part].reshape(shape) for part in range(3))


def solution(mesh):
    tokens = P(None, ("seq", "head"), None)
    placed = P("head", "seq", None)
    return jax.shard_map(
        per_device,
        mesh=mesh,
        in_specs=(
            placed, placed, placed, placed, tokens,
            P("head", None), P("head"), placed, placed, P("head", None, None),
        ),
        out_specs=(tokens, tokens, tokens),
        check_vma=False,
    )
```

```python
import math

import jax
import jax.numpy as jnp
from jax import lax
from jax.experimental import pallas as pl
from jax.experimental.pallas import tpu as pltpu
from jax.sharding import PartitionSpec as P

GROUP = 4
HALF = GROUP // 2
LANES = 128
ACROSS = 4
KEEP_LEVEL = 7
KEEP_SCALE = 8.0 / 7.0
HIGHEST = lax.Precision.HIGHEST
NEG = -1e30


def dot(a, b, dims):
    return lax.dot_general(
        a, b, (dims, ((), ())), precision=HIGHEST, preferred_element_type=jnp.float32
    )


def dot_nt(a, b):
    return dot(a, b, ((1,), (1,)))


def dot_nn(a, b):
    return dot(a, b, ((1,), (0,)))


def dot_tn(a, b):
    return dot(a, b, ((0,), (0,)))


def wide(rows, lanes):
    if lanes <= LANES:
        return rows[:, :lanes]
    return jnp.concatenate([rows] * (lanes // LANES), axis=1)


def row_max(x):
    return jnp.broadcast_to(jnp.max(x, axis=1, keepdims=True), (x.shape[0], LANES))


def row_sum(x):
    return jnp.broadcast_to(jnp.sum(x, axis=1, keepdims=True), (x.shape[0], LANES))


def log_add(a, b):
    return jnp.maximum(a, b) + jnp.log(1.0 + jnp.exp(-jnp.abs(a - b)))


def masked_lse(scores, allowed):
    masked = jnp.where(allowed, scores, NEG)
    top = row_max(masked)
    return top + jnp.log(row_sum(jnp.exp(masked - wide(top, scores.shape[1]))))


def iotas(rows, cols):
    shape = (rows, cols)
    return lax.broadcasted_iota(jnp.int32, shape, 0), lax.broadcasted_iota(jnp.int32, shape, 1)


def spread_matrix(words, first, cols):
    source, column = iotas(4 * words, cols)
    column = column + first
    chosen = (column % 4 == source // words) & (column // 4 == source % words)
    return jnp.where(chosen, 1.0, 0.0).astype(jnp.bfloat16)


def keep_flags(words, axis):
    kept = [
        jnp.where(((words >> (3 * level)) & 7) < KEEP_LEVEL, 1.0, 0.0) for level in range(4)
    ]
    return jnp.concatenate(kept, axis=axis).astype(jnp.bfloat16)


def spread_flags(flags, spread, axis):
    whole = lax.dot_general(
        flags, spread, (((axis,), (0,)), ((), ())), preferred_element_type=jnp.float32
    )
    return whole * jnp.float32(KEEP_SCALE)


def pair_terms(scores, allowed, lse, delta, keep, grad_rows, values):
    cols = scores.shape[1]
    probs = jnp.where(allowed, jnp.exp(scores - wide(lse, cols)), 0.0)
    grad_probs = dot_nt(grad_rows, values) * keep
    return probs * keep, probs * (grad_probs - wide(delta, cols))


def place_info():
    place = lax.axis_index("seq")
    shifted = place + HALF
    return place, shifted // GROUP, shifted % GROUP


def place_masks(place, pos, quarter, rows):
    row, col = iotas(quarter, rows)
    return (col <= pos * quarter + row) & (place - pos + col // quarter >= 0)


def prep_kernel(mid_off, x, o):
    _, segment, pos = place_info()
    heads, rows, _ = x.k.shape
    words = x.drop_mid.shape[2]
    for head in range(heads):
        picked = pl.ds(mid_off[head, segment], rows // GROUP, stride=GROUP)
        mid_q, mid_k, mid_v = x.q[head, picked, :], x.k[head, picked, :], x.v[head, picked, :]
        mid_words = x.drop_mid[head].astype(jnp.float32)
        mid_words = jnp.concatenate([mid_words] * (LANES // words), axis=1)
        o.kv0[0, head] = mid_k
        o.kv0[1, head] = mid_v
        for step, ref in ((1, o.send1), (2, o.send2), (3, o.send3)):
            later = pos + step < GROUP
            ref[0, head] = jnp.where(later, mid_k, mid_q)
            ref[1, head] = jnp.where(later, mid_v, mid_words)


def local_kernel(mid_off, far_off, x, o):
    heads, rows, width = x.q.shape
    row, col = iotas(rows, rows)
    for head in range(heads):
        o.lse[head] = masked_lse(dot_nt(x.q[head], x.k[head]) * (width**-0.5), row >= col)


def gather_mid(x, side, head, buf):
    _, _, pos = place_info()
    quarter = x.kv0.shape[2]
    for distance in range(GROUP):
        start = ((pos - distance) % GROUP) * quarter
        buf[pl.ds(start, quarter), :] = x[f"kv{distance}"][side, head]


def mid_kernel(mid_off, far_off, x, o, buf):
    place, segment, pos = place_info()
    heads, rows, width = x.q.shape
    quarter = rows // GROUP
    count, sends = lax.axis_size("seq"), o.far_send.shape[0]
    far_rows = rows // count
    line = place // (count // sends)
    for head in range(heads):
        o.g[head] = x.g_parts[:, head].reshape(rows, width)
        far = pl.ds(far_off[head], far_rows, stride=count)
        far_q, far_k, far_v = x.q[head, far, :], x.k[head, far, :], x.v[head, far, :]
        far_g = o.g[head, far, :]
        for dest in range(sends):
            o.far_send[dest, head] = far_k
            o.far_send[dest, heads + head] = jnp.where(dest >= line, far_v, far_q)
            o.far_send[dest, 2 * heads + head] = far_g
    allowed = place_masks(place, pos, quarter, rows)
    _, lane = iotas(far_rows, LANES)
    part = lane // (LANES // (2 * heads))
    row_facts = jnp.zeros((far_rows, LANES), jnp.float32)
    for head in range(heads):
        o.delta[head] = row_sum(o.g[head] * x.output[head])
        gather_mid(x, 0, head, buf)
        mid = pl.ds(mid_off[head, segment], quarter, stride=GROUP)
        far = pl.ds(far_off[head], far_rows, stride=count)
        scores = dot_nt(x.q[head, mid, :], buf[...]) * (width**-0.5)
        o.lse[head] = x.lse[head]
        o.lse[head, mid, :] = log_add(x.lse[head, mid, :], masked_lse(scores, allowed))
        row_facts = jnp.where(part == 2 * head, o.lse[head, far, :], row_facts)
        row_facts = jnp.where(part == 2 * head + 1, o.delta[head, far, :], row_facts)
    for dest in range(sends):
        o.far_send[dest, 3 * heads] = row_facts


def relay_kernel(mid_off, far_off, x, o):
    place, _, _ = place_info()
    heads, rows, _ = x.q.shape
    sends = o.relay.shape[0]
    lines = x.column.shape[0]
    for dest in range(sends):
        o.relay[dest] = x.column[...]
    for head in range(heads):
        far_q = x.q[head, pl.ds(far_off[head], rows // (lines * sends), stride=lines * sends), :]
        far_v = x.column[place // sends, heads + head]
        for dest in range(sends):
            o.relay[dest, place // sends, heads + head] = jnp.where(
                dest >= place % sends, far_v, far_q
            )


def rows_kernel(mid_off, far_off, x, o):
    _, segment, _ = place_info()
    heads, rows, width = x.g.shape
    quarter = rows // GROUP
    _, lane = iotas(quarter, LANES)
    part = lane // (LANES // (2 * heads))
    facts = jnp.zeros((quarter, LANES), jnp.float32)
    for head in range(heads):
        mid = pl.ds(mid_off[head, segment], quarter, stride=GROUP)
        o.rows[head] = x.g[head, mid, :]
        facts = jnp.where(part == 2 * head, x.lse[head, mid, :], facts)
        facts = jnp.where(part == 2 * head + 1, x.delta[head, mid, :], facts)
    o.rows[heads] = facts


def terms_kernel(mid_off, far_off, x, o, buf, keep_buf):
    place, segment, pos = place_info()
    heads, rows, width = x.q.shape
    quarter = rows // GROUP
    scale = width**-0.5
    words = x.drop_local.shape[1]
    far_rows = o.far_keep.shape[1]
    key_spread = spread_matrix(words, pos * quarter, quarter)
    spread = spread_matrix(words, 0, rows)
    far_spread = spread_matrix(words, place * far_rows, far_rows)
    for head in range(heads):
        o.scores[head] = dot_nt(x.q[head], x.k[head]) * scale
        keep = spread_flags(keep_flags(x.drop_local[head], 0), spread, 0)
        o.keep[head] = keep
        o.terms[head] = dot_nt(x.g[head], x.v[head]) * keep - wide(x.delta[head], rows)
        mid = pl.ds(mid_off[head, segment], rows // GROUP, stride=GROUP)
        gather_mid(x, 0, head, buf)
        mid_q = x.q[head, mid, :]
        o.mid_k[head] = buf[...]
        o.mid_scores[head] = dot_nt(mid_q, buf[...]) * scale
        own_block = pl.ds(pos * quarter, quarter)
        buf[own_block, :] = mid_q
        o.key_pairs[head, :, 0:quarter] = dot_nt(buf[...], x.kv0[0, head]) * scale
        gather_mid(x, 1, head, buf)
        keep_buf[:, 0:words] = buf[:, 0:words]
        keep_buf[own_block, 0:words] = x.drop_mid[head].astype(jnp.float32)
        flags = keep_flags(keep_buf[:, 0:words].astype(jnp.int32), 1)
        o.key_pairs[head, :, quarter : 2 * quarter] = spread_flags(flags, key_spread, 1)
        keep = spread_flags(keep_flags(x.drop_mid[head], 1), spread, 1)
        o.mid_terms[head] = dot_nt(x.g[head, mid, :], buf[...]) * keep - wide(
            x.delta[head, mid, :], rows
        )
        flags = keep_flags(x.drop_far[head], 0)
        keep_buf[...] = spread_flags(flags, spread, 0)
        o.far_keep[head] = keep_buf[pl.ds(place * far_rows, far_rows), :]
        o.far_cols[:, head * far_rows : (head + 1) * far_rows] = spread_flags(flags, far_spread, 0)


def fact(facts, index, share):
    return jnp.broadcast_to(facts[:, index * share : index * share + 1], facts.shape)


def grad_kernel(
    mid_off, far_off, x, o, q_buf, lse_buf, far_lse, key_lse, gq_buf, gk_buf, gv_buf, mid_g,
    key_delta, score_buf, far_ref,
):
    place, segment, pos = place_info()
    heads, rows, width = x.q.shape
    quarter = rows // GROUP
    parts = o.stacked.shape[0]
    count = far_ref.shape[0]
    across, lines = x.far.shape[:2]
    for source in range(count):
        far_ref[source] = x.far[source % across, source // across]
    far_rows = rows // count
    scale = width**-0.5
    share = LANES // (2 * heads)
    row, col = iotas(rows, rows)
    causal = row >= col
    far_row, far_col = iotas(far_rows, rows)
    far_allowed = far_col <= place * far_rows + far_row
    key_row, key_col = iotas(rows, far_rows)
    far_key_allowed = place * far_rows + key_col <= key_row
    mid_allowed = place_masks(place, pos, quarter, rows)
    mid_row, mid_col = iotas(rows, quarter)
    block = mid_row // quarter
    mid_key_allowed = ((block > pos) & (place - pos + block < count)) | (
        (block == pos) & (mid_row % quarter >= mid_col)
    )
    own_block = pl.ds(pos * quarter, quarter)
    facts = far_ref[:, 3 * heads].reshape(rows, LANES)
    own = pl.ds(place * far_rows, far_rows)
    for head in range(heads):
        mid_start = mid_off[head, segment]
        mid = pl.ds(mid_start, quarter, stride=GROUP)
        far = pl.ds(far_off[head], far_rows, stride=count)
        all_k = far_ref[:, head].reshape(rows, width)
        all_v = far_ref[:, heads + head].reshape(rows, width)
        all_g = far_ref[:, 2 * heads + head].reshape(rows, width)
        far_q = x.q[head, far, :]
        q_buf[...] = all_v
        q_buf[own, :] = far_q
        all_q = q_buf[...]
        score_buf[...] = dot_nt(all_q, all_k) * scale
        far_lse[...] = log_add(fact(facts, 2 * head, share), masked_lse(score_buf[...], causal))
        lse_buf[...] = x.lse[head]
        lse_buf[far, :] = far_lse[own, :]

        probs = jnp.where(causal, jnp.exp(x.scores[head] - wide(lse_buf[...], rows)), 0.0)
        grad_scores = probs * x.terms[head]
        gq_buf[...] = dot_nn(grad_scores, x.k[head]) * scale
        gk_buf[...] = dot_tn(grad_scores, x.q[head]) * scale
        gv_buf[...] = dot_tn(probs * x.keep[head], x.g[head])

        probs = jnp.where(
            mid_allowed, jnp.exp(x.mid_scores[head] - wide(lse_buf[mid, :], rows)), 0.0
        )
        grad_scores = probs * x.mid_terms[head]
        gq_buf[mid, :] = gq_buf[mid, :] + dot_nn(grad_scores, x.mid_k[head]) * scale

        dropped, grad_scores = pair_terms(
            score_buf[own, :], far_allowed, lse_buf[far, :],
            fact(far_ref[place, 3 * heads], 2 * head + 1, share),
            x.far_keep[head], far_ref[place, 2 * heads + head], all_v,
        )
        gq_buf[far, :] = gq_buf[far, :] + dot_nn(grad_scores, all_k) * scale
        o.stacked[:, 0, head] = gq_buf[...].reshape(parts, rows // parts, width)

        meets = far_off[head] % GROUP == mid_start
        first = jnp.where(meets, (far_off[head] - mid_start) // GROUP, 0)
        for step in range(GROUP):
            source = (pos + step) % GROUP
            part = pl.ds(source * quarter, quarter)
            rows_ref = x[f"rows{(GROUP - step) % GROUP}"]
            mid_g[part, :] = rows_ref[head]
            key_delta[part, :] = fact(rows_ref[heads], 2 * head + 1, share)
            if step == 0:
                key_lse[part, :] = lse_buf[mid, :]
                continue
            key_lse[part, :] = fact(rows_ref[heads], 2 * head, share)
            spots = pl.ds(source * quarter + first, far_rows, stride=count // GROUP)
            start = jnp.clip(place - pos + source, 0, count - 1) * far_rows
            key_lse[spots, :] = jnp.where(
                meets, far_lse[pl.ds(start, far_rows), :], key_lse[spots, :]
            )
        q_buf[...] = x.mid_k[head]
        q_buf[own_block, :] = x.q[head, mid, :]
        probs = jnp.where(
            mid_key_allowed, jnp.exp(x.key_pairs[head, :, 0:quarter] - key_lse[:, 0:quarter]), 0.0
        )
        keep = x.key_pairs[head, :, quarter : 2 * quarter]
        grad_scores = probs * (
            dot_nt(mid_g[...], x.kv0[1, head]) * keep - key_delta[:, 0:quarter]
        )
        gk_buf[mid, :] = gk_buf[mid, :] + dot_tn(grad_scores, q_buf[...]) * scale
        gv_buf[mid, :] = gv_buf[mid, :] + dot_tn(probs * keep, mid_g[...])

        far_k, far_v = far_ref[place, head], far_ref[place, heads + head]
        dropped, grad_scores = pair_terms(
            dot_nt(all_q, far_k) * scale, far_key_allowed, far_lse[...],
            fact(facts, 2 * head + 1, share),
            x.far_cols[:, head * far_rows : (head + 1) * far_rows], all_g, far_v,
        )
        gk_buf[far, :] = gk_buf[far, :] + dot_tn(grad_scores, all_q) * scale
        gv_buf[far, :] = gv_buf[far, :] + dot_tn(dropped, all_g)
        o.stacked[:, 1, head] = gk_buf[...].reshape(parts, rows // parts, width)
        o.stacked[:, 2, head] = gv_buf[...].reshape(parts, rows // parts, width)


class Fetched:
    def __init__(self, copies, ref):
        self.copies, self.ref, self.shape, self.seen = copies, ref, ref.shape, set()

    def wait(self, head):
        if head not in self.seen:
            self.seen.add(head)
            self.copies[head].wait()

    def __getitem__(self, index):
        leading = index[0] if isinstance(index, tuple) else index
        for head in range(len(self.copies)):
            if len(self.copies) == 1 or not isinstance(leading, int) or leading == head:
                self.wait(head)
        return self.ref[index]


class Loaded:
    def __init__(self, refs):
        self.__dict__.update(refs=refs)

    def __getitem__(self, name):
        return self.refs[name]

    def __getattr__(self, name):
        return self.refs[name]


class Stored:
    def __init__(self, refs, sends):
        self.__dict__.update(refs, sends=sends)

    def send(self, name, part=slice(None)):
        self.sends(name, part)


def call(kernel, scalars, arrays, outs, scratch=(), flops=0, fetched=()):
    heads = 2
    names = list(arrays)
    loads = [name for name in names if name in fetched]
    out_names = [name.rstrip("+") for name in outs]
    shapes = dict(zip(out_names, outs.values()))
    saves = [name for name in outs if not name.endswith("+")]
    hbm, vmem = pl.BlockSpec(memory_space=pltpu.HBM), pl.BlockSpec(memory_space=pltpu.VMEM)

    def run(*refs):
        refs = list(refs)

        def take(count):
            taken, refs[:] = refs[:count], refs[count:]
            return taken

        scalar_refs, in_refs, out_refs = take(len(scalars)), take(len(names)), take(len(outs))
        in_bufs, out_bufs, extra = take(len(loads)), take(len(saves)), take(len(scratch))
        in_sems, out_sems = refs
        given, written = dict(zip(names, in_refs)), dict(zip(out_names, out_refs))
        copies = {name: {} for name in loads}
        used = 0
        for head in range(heads):
            for name, buf in zip(loads, in_bufs):
                whole = buf.shape[0] != heads
                if whole and head:
                    continue
                part = slice(None) if whole else head
                copy = pltpu.make_async_copy(given[name].at[part], buf.at[part], in_sems.at[used])
                copy.start()
                copies[name][head] = copy
                used += 1
        moving = {name: Fetched(copies[name], buf) for name, buf in zip(loads, in_bufs)}
        loaded = Loaded({**given, **moving})
        buffers = dict(zip(saves, out_bufs))
        writes = []

        def send(name, part=slice(None)):
            write = pltpu.make_async_copy(
                buffers[name].at[part], written[name].at[part], out_sems.at[len(writes)]
            )
            write.start()
            writes.append(write)
            sent.add(name)

        sent = set()
        kernel(*scalar_refs, loaded, Stored({**written, **buffers}, send), *extra)
        for name in loads:
            for head in copies[name]:
                moving[name].wait(head)
        for name in saves:
            if name not in sent:
                send(name)
        for write in writes:
            write.wait()

    values = list(arrays.values())
    moved = 4 * sum(math.prod(shape) for shape in [v.shape for v in values] + [*shapes.values()])
    result = pl.pallas_call(
        run,
        out_shape=[
            pltpu.HBM(shape, jnp.float32)
            if name in saves
            else jax.ShapeDtypeStruct(shape, jnp.float32)
            for name, shape in shapes.items()
        ],
        in_specs=[pl.BlockSpec(memory_space=pltpu.SMEM)] * len(scalars)
        + [hbm if name in loads else vmem for name in names],
        out_specs=[hbm if name in saves else vmem for name in shapes],
        scratch_shapes=[pltpu.VMEM(arrays[name].shape, arrays[name].dtype) for name in loads]
        + [pltpu.VMEM(shapes[name], jnp.float32) for name in saves]
        + [pltpu.VMEM(shape, jnp.float32) for shape in scratch]
        + [
            pltpu.SemaphoreType.DMA((max(heads * len(loads), 1),)),
            pltpu.SemaphoreType.DMA((max(2 * len(saves), 1),)),
        ],
        cost_estimate=pl.CostEstimate(flops=flops, transcendentals=0, bytes_accessed=moved),
        compiler_params=pltpu.CompilerParams(vmem_limit_bytes=40 * 1024 * 1024),
    )(
        *scalars,
        *[
            pltpu.with_memory_space_constraint(value, pltpu.HBM) if name in loads else value
            for name, value in arrays.items()
        ],
    )
    return dict(zip(out_names, result))


def turned(value, steps):
    count = lax.axis_size("seq")
    pairs = []
    for first in range(-HALF, count - HALF, GROUP):
        for pos in range(GROUP):
            pairs.append(((first + pos) % count, (first + (pos + steps) % GROUP) % count))
    return lax.ppermute(value, "seq", pairs)


def exchange(value, axis, groups=None):
    return lax.all_to_all(
        value, axis, split_axis=0, concat_axis=0, tiled=True, axis_index_groups=groups
    )


def per_device(q, k, v, output, grad_output, mid_off, far_off, drop_local, drop_mid, drop_far):
    heads, rows, width = q.shape
    count = lax.axis_size("seq")
    parts = lax.axis_size("head")
    quarter = rows // GROUP
    far_rows = rows // count
    whole = (heads, rows, width)
    pairs = (heads, rows, rows)
    mid_pairs = (heads, quarter, rows)
    key_pairs = (heads, rows, quarter)
    block = 6 * 2 * heads * rows * rows * width
    drop_local = jnp.swapaxes(drop_local, 1, 2)
    drop_far = jnp.swapaxes(drop_far, 1, 2)
    offsets = (mid_off, far_off)
    lines = count // ACROSS
    rows_of = [[line * ACROSS + i for i in range(ACROSS)] for line in range(lines)]
    columns = [list(group) for group in zip(*rows_of)]

    g_parts = exchange(grad_output.reshape(parts, heads, rows // parts, width), "head")
    first = call(
        prep_kernel,
        (mid_off,),
        {"q": q, "k": k, "v": v, "drop_mid": drop_mid},
        {f"{name}+": (2, heads, quarter, width) for name in ("kv0", "send1", "send2", "send3")},
        fetched=("v", "drop_mid"),
    )
    kv = {
        f"kv{step}": turned(first[f"send{step}"], step) if step else first["kv0"]
        for step in range(GROUP)
    }
    lse = call(local_kernel, offsets, {"q": q, "k": k}, {"lse+": whole}, flops=block)["lse"]
    mid = call(
        mid_kernel,
        offsets,
        {"g_parts": g_parts, "q": q, "k": k, "v": v, **kv, "output": output, "lse": lse},
        {
            "g+": whole,
            "delta+": whole,
            "lse+": whole,
            "far_send+": (lines, 3 * heads + 1, far_rows, width),
        },
        scratch=((rows, width),),
        flops=block // GROUP,
    )
    column = exchange(mid.pop("far_send"), "seq", columns)
    own_rows = call(
        rows_kernel, offsets, mid, {"rows+": (heads + 1, quarter, width)}
    )["rows"]
    mid_rows = {
        f"rows{step}": turned(own_rows, step) if step else own_rows for step in range(GROUP)
    }
    term_shapes = {
        "scores": pairs,
        "terms": pairs,
        "keep": pairs,
        "mid_scores": mid_pairs,
        "mid_terms": mid_pairs,
        "mid_k": whole,
        "far_keep": (heads, far_rows, rows),
        "key_pairs": whole,
        "far_cols": (rows, heads * far_rows),
    }
    terms = call(
        terms_kernel,
        offsets,
        {
            "q": q, "k": k, "v": v, "g": mid["g"], "delta": mid["delta"], **kv,
            "drop_local": drop_local, "drop_mid": drop_mid, "drop_far": drop_far,
        },
        term_shapes,
        scratch=((rows, width), (rows, rows)),
        flops=2 * block,
    )
    column, own_rows, terms = lax.optimization_barrier((column, own_rows, terms))
    relay = call(
        relay_kernel,
        offsets,
        {"column": column, "q": q},
        {"relay+": (ACROSS, lines, 3 * heads + 1, far_rows, width)},
    )["relay"]
    far = exchange(relay, "seq", rows_of)
    stacked = call(
        grad_kernel,
        offsets,
        {
            "far": far, "q": q, "k": k, "g": mid["g"], "lse": mid["lse"],
            **{name: terms[name] for name in term_shapes}, **mid_rows, "kv0": kv["kv0"],
        },
        {"stacked+": (parts, 3, heads, rows // parts, width)},
        scratch=((rows, width),) * 9
        + ((rows, rows), (count, 3 * heads + 1, far_rows, width)),
        flops=8 * block,
        fetched=("k", "rows1", "rows2", "rows3", *terms),
    )["stacked"]
    result = exchange(stacked, "head")
    shape = (parts * heads, rows // parts, width)
    return tuple(result[:, part].reshape(shape) for part in range(3))


def solution(mesh):
    tokens = P(None, ("seq", "head"), None)
    placed = P("head", "seq", None)
    return jax.shard_map(
        per_device,
        mesh=mesh,
        in_specs=(
            placed, placed, placed, placed, tokens,
            P("head", None), P("head"), placed, placed, P("head", None, None),
        ),
        out_specs=(tokens, tokens, tokens),
        check_vma=False,
    )
```

```python
import math

import jax
import jax.numpy as jnp
from jax import lax
from jax.experimental import pallas as pl
from jax.experimental.pallas import tpu as pltpu
from jax.sharding import PartitionSpec as P

GROUP = 4
HALF = GROUP // 2
LANES = 128
ACROSS = 4
KEEP_LEVEL = 7
KEEP_SCALE = 8.0 / 7.0
HIGHEST = lax.Precision.HIGHEST
NEG = -1e30


def dot(a, b, dims):
    return lax.dot_general(
        a, b, (dims, ((), ())), precision=HIGHEST, preferred_element_type=jnp.float32
    )


def dot_nt(a, b):
    return dot(a, b, ((1,), (1,)))


def dot_nn(a, b):
    return dot(a, b, ((1,), (0,)))


def dot_tn(a, b):
    return dot(a, b, ((0,), (0,)))


def wide(rows, lanes):
    if lanes <= LANES:
        return rows[:, :lanes]
    return jnp.concatenate([rows] * (lanes // LANES), axis=1)


def row_max(x):
    return jnp.broadcast_to(jnp.max(x, axis=1, keepdims=True), (x.shape[0], LANES))


def row_sum(x):
    return jnp.broadcast_to(jnp.sum(x, axis=1, keepdims=True), (x.shape[0], LANES))


def log_add(a, b):
    return jnp.maximum(a, b) + jnp.log(1.0 + jnp.exp(-jnp.abs(a - b)))


def masked_lse(scores, allowed):
    masked = jnp.where(allowed, scores, NEG)
    top = row_max(masked)
    return top + jnp.log(row_sum(jnp.exp(masked - wide(top, scores.shape[1]))))


def iotas(rows, cols):
    shape = (rows, cols)
    return lax.broadcasted_iota(jnp.int32, shape, 0), lax.broadcasted_iota(jnp.int32, shape, 1)


def spread_matrix(words, first, cols):
    source, column = iotas(4 * words, cols)
    column = column + first
    chosen = (column % 4 == source // words) & (column // 4 == source % words)
    return jnp.where(chosen, 1.0, 0.0).astype(jnp.bfloat16)


def keep_flags(words, axis):
    kept = [
        jnp.where(((words >> (3 * level)) & 7) < KEEP_LEVEL, 1.0, 0.0) for level in range(4)
    ]
    return jnp.concatenate(kept, axis=axis).astype(jnp.bfloat16)


def spread_flags(flags, spread, axis):
    whole = lax.dot_general(
        flags, spread, (((axis,), (0,)), ((), ())), preferred_element_type=jnp.float32
    )
    return whole * jnp.float32(KEEP_SCALE)


def pair_terms(scores, allowed, lse, delta, keep, grad_rows, values):
    cols = scores.shape[1]
    probs = jnp.where(allowed, jnp.exp(scores - wide(lse, cols)), 0.0)
    grad_probs = dot_nt(grad_rows, values) * keep
    return probs * keep, probs * (grad_probs - wide(delta, cols))


def place_info():
    place = lax.axis_index("seq")
    shifted = place + HALF
    return place, shifted // GROUP, shifted % GROUP


def place_masks(place, pos, quarter, rows):
    row, col = iotas(quarter, rows)
    return (col <= pos * quarter + row) & (place - pos + col // quarter >= 0)


def prep_kernel(mid_off, x, o):
    _, segment, pos = place_info()
    heads, rows, _ = x.k.shape
    words = x.drop_mid.shape[2]
    for head in range(heads):
        picked = pl.ds(mid_off[head, segment], rows // GROUP, stride=GROUP)
        mid_q, mid_k, mid_v = x.q[head, picked, :], x.k[head, picked, :], x.v[head, picked, :]
        mid_words = x.drop_mid[head].astype(jnp.float32)
        mid_words = jnp.concatenate([mid_words] * (LANES // words), axis=1)
        o.kv0[0, head] = mid_k
        o.kv0[1, head] = mid_v
        for step, ref in ((1, o.send1), (2, o.send2), (3, o.send3)):
            later = pos + step < GROUP
            ref[0, head] = jnp.where(later, mid_k, mid_q)
            ref[1, head] = jnp.where(later, mid_v, mid_words)


def local_kernel(mid_off, far_off, x, o):
    heads, rows, width = x.q.shape
    row, col = iotas(rows, rows)
    for head in range(heads):
        o.lse[head] = masked_lse(dot_nt(x.q[head], x.k[head]) * (width**-0.5), row >= col)


def gather_mid(x, side, head, buf):
    _, _, pos = place_info()
    quarter = x.kv0.shape[2]
    for distance in range(GROUP):
        start = ((pos - distance) % GROUP) * quarter
        buf[pl.ds(start, quarter), :] = x[f"kv{distance}"][side, head]


def mid_kernel(mid_off, far_off, x, o, buf):
    place, segment, pos = place_info()
    heads, rows, width = x.q.shape
    quarter = rows // GROUP
    count, sends = lax.axis_size("seq"), o.far_send.shape[0]
    far_rows = rows // count
    line = place // (count // sends)
    for head in range(heads):
        o.g[head] = x.g_parts[:, head].reshape(rows, width)
        far = pl.ds(far_off[head], far_rows, stride=count)
        far_q, far_k, far_v = x.q[head, far, :], x.k[head, far, :], x.v[head, far, :]
        far_g = o.g[head, far, :]
        for dest in range(sends):
            o.far_send[dest, head] = far_k
            o.far_send[dest, heads + head] = jnp.where(dest >= line, far_v, far_q)
            o.far_send[dest, 2 * heads + head] = far_g
    allowed = place_masks(place, pos, quarter, rows)
    _, lane = iotas(far_rows, LANES)
    part = lane // (LANES // (2 * heads))
    row_facts = jnp.zeros((far_rows, LANES), jnp.float32)
    for head in range(heads):
        o.delta[head] = row_sum(o.g[head] * x.output[head])
        gather_mid(x, 0, head, buf)
        mid = pl.ds(mid_off[head, segment], quarter, stride=GROUP)
        far = pl.ds(far_off[head], far_rows, stride=count)
        scores = dot_nt(x.q[head, mid, :], buf[...]) * (width**-0.5)
        o.lse[head] = x.lse[head]
        o.lse[head, mid, :] = log_add(x.lse[head, mid, :], masked_lse(scores, allowed))
        row_facts = jnp.where(part == 2 * head, o.lse[head, far, :], row_facts)
        row_facts = jnp.where(part == 2 * head + 1, o.delta[head, far, :], row_facts)
    for dest in range(sends):
        o.far_send[dest, 3 * heads] = row_facts


def relay_kernel(mid_off, far_off, x, o):
    place, _, _ = place_info()
    heads, rows, _ = x.q.shape
    sends = o.relay.shape[0]
    lines = x.column.shape[0]
    for dest in range(sends):
        o.relay[dest] = x.column[...]
    for head in range(heads):
        far_q = x.q[head, pl.ds(far_off[head], rows // (lines * sends), stride=lines * sends), :]
        far_v = x.column[place // sends, heads + head]
        for dest in range(sends):
            o.relay[dest, place // sends, heads + head] = jnp.where(
                dest >= place % sends, far_v, far_q
            )


def rows_kernel(mid_off, far_off, x, o):
    _, segment, _ = place_info()
    heads, rows, width = x.g.shape
    quarter = rows // GROUP
    _, lane = iotas(quarter, LANES)
    part = lane // (LANES // (2 * heads))
    facts = jnp.zeros((quarter, LANES), jnp.float32)
    for head in range(heads):
        mid = pl.ds(mid_off[head, segment], quarter, stride=GROUP)
        o.rows[head] = x.g[head, mid, :]
        facts = jnp.where(part == 2 * head, x.lse[head, mid, :], facts)
        facts = jnp.where(part == 2 * head + 1, x.delta[head, mid, :], facts)
    o.rows[heads] = facts


def terms_kernel(mid_off, far_off, x, o, buf, keep_buf):
    place, segment, pos = place_info()
    heads, rows, width = x.q.shape
    quarter = rows // GROUP
    scale = width**-0.5
    words = x.drop_local.shape[1]
    far_rows = o.far_keep.shape[1]
    key_spread = spread_matrix(words, pos * quarter, quarter)
    spread = spread_matrix(words, 0, rows)
    far_spread = spread_matrix(words, place * far_rows, far_rows)
    for head in range(heads):
        o.scores[head] = dot_nt(x.q[head], x.k[head]) * scale
        keep = spread_flags(keep_flags(x.drop_local[head], 0), spread, 0)
        o.keep[head] = keep
        o.terms[head] = dot_nt(x.g[head], x.v[head]) * keep - wide(x.delta[head], rows)
        mid = pl.ds(mid_off[head, segment], rows // GROUP, stride=GROUP)
        gather_mid(x, 0, head, buf)
        mid_q = x.q[head, mid, :]
        o.mid_k[head] = buf[...]
        o.mid_scores[head] = dot_nt(mid_q, buf[...]) * scale
        own_block = pl.ds(pos * quarter, quarter)
        buf[own_block, :] = mid_q
        o.key_pairs[head, :, 0:quarter] = dot_nt(buf[...], x.kv0[0, head]) * scale
        gather_mid(x, 1, head, buf)
        keep_buf[:, 0:words] = buf[:, 0:words]
        keep_buf[own_block, 0:words] = x.drop_mid[head].astype(jnp.float32)
        flags = keep_flags(keep_buf[:, 0:words].astype(jnp.int32), 1)
        o.key_pairs[head, :, quarter : 2 * quarter] = spread_flags(flags, key_spread, 1)
        keep = spread_flags(keep_flags(x.drop_mid[head], 1), spread, 1)
        o.mid_terms[head] = dot_nt(x.g[head, mid, :], buf[...]) * keep - wide(
            x.delta[head, mid, :], rows
        )
        flags = keep_flags(x.drop_far[head], 0)
        keep_buf[...] = spread_flags(flags, spread, 0)
        o.far_keep[head] = keep_buf[pl.ds(place * far_rows, far_rows), :]
        o.far_cols[:, head * far_rows : (head + 1) * far_rows] = spread_flags(flags, far_spread, 0)


def fact(facts, index, share):
    return jnp.broadcast_to(facts[:, index * share : index * share + 1], facts.shape)


def grad_kernel(
    mid_off, far_off, x, o, q_buf, lse_buf, far_lses, key_lse, gq_buf, gk_buf, gv_buf, mid_g,
    key_delta, score_buf, far_ref,
):
    place, segment, pos = place_info()
    heads, rows, width = x.q.shape
    quarter = rows // GROUP
    parts = o.stacked.shape[0]
    count = far_ref.shape[0]
    across, lines = x.far.shape[:2]
    for source in range(count):
        far_ref[source] = x.far[source % across, source // across]
    far_rows = rows // count
    scale = width**-0.5
    share = LANES // (2 * heads)
    row, col = iotas(rows, rows)
    causal = row >= col
    far_row, far_col = iotas(far_rows, rows)
    far_allowed = far_col <= place * far_rows + far_row
    key_row, key_col = iotas(rows, far_rows)
    far_key_allowed = place * far_rows + key_col <= key_row
    mid_allowed = place_masks(place, pos, quarter, rows)
    mid_row, mid_col = iotas(rows, quarter)
    block = mid_row // quarter
    mid_key_allowed = ((block > pos) & (place - pos + block < count)) | (
        (block == pos) & (mid_row % quarter >= mid_col)
    )
    own_block = pl.ds(pos * quarter, quarter)
    facts = far_ref[:, 3 * heads].reshape(rows, LANES)
    own = pl.ds(place * far_rows, far_rows)
    for head in range(heads):
        far = pl.ds(far_off[head], far_rows, stride=count)
        q_buf[...] = far_ref[:, heads + head].reshape(rows, width)
        q_buf[own, :] = x.q[head, far, :]
        all_k = far_ref[:, head].reshape(rows, width)
        score_buf[head] = dot_nt(q_buf[...], all_k) * scale
        far_lses[head] = log_add(
            fact(facts, 2 * head, share), masked_lse(score_buf[head], causal)
        )
    for head in range(heads):
        mid_start = mid_off[head, segment]
        mid = pl.ds(mid_start, quarter, stride=GROUP)
        far = pl.ds(far_off[head], far_rows, stride=count)
        all_k = far_ref[:, head].reshape(rows, width)
        all_v = far_ref[:, heads + head].reshape(rows, width)
        all_g = far_ref[:, 2 * heads + head].reshape(rows, width)
        q_buf[...] = all_v
        q_buf[own, :] = x.q[head, far, :]
        all_q = q_buf[...]
        far_lse = far_lses.at[head]
        lse_buf[...] = x.lse[head]
        lse_buf[far, :] = far_lse[own, :]

        probs = jnp.where(causal, jnp.exp(x.scores[head] - wide(lse_buf[...], rows)), 0.0)
        grad_scores = probs * x.terms[head]
        gq_buf[...] = dot_nn(grad_scores, x.k[head]) * scale
        gk_buf[...] = dot_tn(grad_scores, x.q[head]) * scale
        gv_buf[...] = dot_tn(probs * x.keep[head], x.g[head])

        probs = jnp.where(
            mid_allowed, jnp.exp(x.mid_scores[head] - wide(lse_buf[mid, :], rows)), 0.0
        )
        grad_scores = probs * x.mid_terms[head]
        gq_buf[mid, :] = gq_buf[mid, :] + dot_nn(grad_scores, x.mid_k[head]) * scale

        dropped, grad_scores = pair_terms(
            score_buf[head, own, :], far_allowed, lse_buf[far, :],
            fact(far_ref[place, 3 * heads], 2 * head + 1, share),
            x.far_keep[head], far_ref[place, 2 * heads + head], all_v,
        )
        gq_buf[far, :] = gq_buf[far, :] + dot_nn(grad_scores, all_k) * scale
        o.stacked[:, 0, head] = gq_buf[...].reshape(parts, rows // parts, width)

        meets = far_off[head] % GROUP == mid_start
        first = jnp.where(meets, (far_off[head] - mid_start) // GROUP, 0)
        for step in range(GROUP):
            source = (pos + step) % GROUP
            part = pl.ds(source * quarter, quarter)
            rows_ref = x[f"rows{(GROUP - step) % GROUP}"]
            mid_g[part, :] = rows_ref[head]
            key_delta[part, :] = fact(rows_ref[heads], 2 * head + 1, share)
            if step == 0:
                key_lse[part, :] = lse_buf[mid, :]
                continue
            key_lse[part, :] = fact(rows_ref[heads], 2 * head, share)
            spots = pl.ds(source * quarter + first, far_rows, stride=count // GROUP)
            start = jnp.clip(place - pos + source, 0, count - 1) * far_rows
            key_lse[spots, :] = jnp.where(
                meets, far_lse[pl.ds(start, far_rows), :], key_lse[spots, :]
            )
        q_buf[...] = x.mid_k[head]
        q_buf[own_block, :] = x.q[head, mid, :]
        probs = jnp.where(
            mid_key_allowed, jnp.exp(x.key_pairs[head, :, 0:quarter] - key_lse[:, 0:quarter]), 0.0
        )
        keep = x.key_pairs[head, :, quarter : 2 * quarter]
        grad_scores = probs * (
            dot_nt(mid_g[...], x.kv0[1, head]) * keep - key_delta[:, 0:quarter]
        )
        gk_buf[mid, :] = gk_buf[mid, :] + dot_tn(grad_scores, q_buf[...]) * scale
        gv_buf[mid, :] = gv_buf[mid, :] + dot_tn(probs * keep, mid_g[...])

        far_k, far_v = far_ref[place, head], far_ref[place, heads + head]
        dropped, grad_scores = pair_terms(
            dot_nt(all_q, far_k) * scale, far_key_allowed, far_lse[...],
            fact(facts, 2 * head + 1, share),
            x.far_cols[:, head * far_rows : (head + 1) * far_rows], all_g, far_v,
        )
        gk_buf[far, :] = gk_buf[far, :] + dot_tn(grad_scores, all_q) * scale
        gv_buf[far, :] = gv_buf[far, :] + dot_tn(dropped, all_g)
        o.stacked[:, 1, head] = gk_buf[...].reshape(parts, rows // parts, width)
        o.stacked[:, 2, head] = gv_buf[...].reshape(parts, rows // parts, width)


class Fetched:
    def __init__(self, ref, arrive):
        self.ref, self.shape, self.arrive = ref, ref.shape, arrive

    def __getitem__(self, index):
        self.arrive()
        return self.ref[index]


class Loaded:
    def __init__(self, refs):
        self.__dict__.update(refs=refs)

    def __getitem__(self, name):
        return self.refs[name]

    def __getattr__(self, name):
        return self.refs[name]


class Stored:
    def __init__(self, refs, sends):
        self.__dict__.update(refs, sends=sends)

    def send(self, name, part=slice(None)):
        self.sends(name, part)


def call(kernel, scalars, arrays, outs, scratch=(), flops=0, fetched=()):
    names = list(arrays)
    loads = [name for name in names if name in fetched]
    out_names = [name.rstrip("+") for name in outs]
    shapes = dict(zip(out_names, outs.values()))
    saves = [name for name in outs if not name.endswith("+")]
    hbm, vmem = pl.BlockSpec(memory_space=pltpu.HBM), pl.BlockSpec(memory_space=pltpu.VMEM)

    def run(*refs):
        refs = list(refs)

        def take(count):
            taken, refs[:] = refs[:count], refs[count:]
            return taken

        scalar_refs, in_refs, out_refs = take(len(scalars)), take(len(names)), take(len(outs))
        in_bufs, out_bufs, extra = take(len(loads)), take(len(saves)), take(len(scratch))
        in_sems, out_sems = refs
        given, written = dict(zip(names, in_refs)), dict(zip(out_names, out_refs))
        copies = [
            pltpu.make_async_copy(given[name], buf, in_sems.at[i])
            for i, (name, buf) in enumerate(zip(loads, in_bufs))
        ]
        for copy in copies:
            copy.start()

        def arrive():
            while copies:
                copies.pop(0).wait()

        loaded = Loaded(
            {**given, **{name: Fetched(buf, arrive) for name, buf in zip(loads, in_bufs)}}
        )
        buffers = dict(zip(saves, out_bufs))
        writes = []

        def send(name, part=slice(None)):
            write = pltpu.make_async_copy(
                buffers[name].at[part], written[name].at[part], out_sems.at[len(writes)]
            )
            write.start()
            writes.append(write)
            sent.add(name)

        sent = set()
        kernel(*scalar_refs, loaded, Stored({**written, **buffers}, send), *extra)
        arrive()
        for name in saves:
            if name not in sent:
                send(name)
        for write in writes:
            write.wait()

    values = list(arrays.values())
    moved = 4 * sum(math.prod(shape) for shape in [v.shape for v in values] + [*shapes.values()])
    result = pl.pallas_call(
        run,
        out_shape=[
            pltpu.HBM(shape, jnp.float32)
            if name in saves
            else jax.ShapeDtypeStruct(shape, jnp.float32)
            for name, shape in shapes.items()
        ],
        in_specs=[pl.BlockSpec(memory_space=pltpu.SMEM)] * len(scalars)
        + [hbm if name in loads else vmem for name in names],
        out_specs=[hbm if name in saves else vmem for name in shapes],
        scratch_shapes=[pltpu.VMEM(arrays[name].shape, arrays[name].dtype) for name in loads]
        + [pltpu.VMEM(shapes[name], jnp.float32) for name in saves]
        + [pltpu.VMEM(shape, jnp.float32) for shape in scratch]
        + [
            pltpu.SemaphoreType.DMA((max(len(loads), 1),)),
            pltpu.SemaphoreType.DMA((max(2 * len(saves), 1),)),
        ],
        cost_estimate=pl.CostEstimate(flops=flops, transcendentals=0, bytes_accessed=moved),
        compiler_params=pltpu.CompilerParams(vmem_limit_bytes=40 * 1024 * 1024),
    )(
        *scalars,
        *[
            pltpu.with_memory_space_constraint(value, pltpu.HBM) if name in loads else value
            for name, value in arrays.items()
        ],
    )
    return dict(zip(out_names, result))


def turned(value, steps):
    count = lax.axis_size("seq")
    pairs = []
    for first in range(-HALF, count - HALF, GROUP):
        for pos in range(GROUP):
            pairs.append(((first + pos) % count, (first + (pos + steps) % GROUP) % count))
    return lax.ppermute(value, "seq", pairs)


def exchange(value, axis, groups=None):
    return lax.all_to_all(
        value, axis, split_axis=0, concat_axis=0, tiled=True, axis_index_groups=groups
    )


def per_device(q, k, v, output, grad_output, mid_off, far_off, drop_local, drop_mid, drop_far):
    heads, rows, width = q.shape
    count = lax.axis_size("seq")
    parts = lax.axis_size("head")
    quarter = rows // GROUP
    far_rows = rows // count
    whole = (heads, rows, width)
    pairs = (heads, rows, rows)
    mid_pairs = (heads, quarter, rows)
    key_pairs = (heads, rows, quarter)
    block = 6 * 2 * heads * rows * rows * width
    drop_local = jnp.swapaxes(drop_local, 1, 2)
    drop_far = jnp.swapaxes(drop_far, 1, 2)
    offsets = (mid_off, far_off)
    lines = count // ACROSS
    rows_of = [[line * ACROSS + i for i in range(ACROSS)] for line in range(lines)]
    columns = [list(group) for group in zip(*rows_of)]

    g_parts = exchange(grad_output.reshape(parts, heads, rows // parts, width), "head")
    first = call(
        prep_kernel,
        (mid_off,),
        {"q": q, "k": k, "v": v, "drop_mid": drop_mid},
        {f"{name}+": (2, heads, quarter, width) for name in ("kv0", "send1", "send2", "send3")},
        fetched=("v", "drop_mid"),
    )
    kv = {
        f"kv{step}": turned(first[f"send{step}"], step) if step else first["kv0"]
        for step in range(GROUP)
    }
    lse = call(local_kernel, offsets, {"q": q, "k": k}, {"lse+": whole}, flops=block)["lse"]
    mid = call(
        mid_kernel,
        offsets,
        {"g_parts": g_parts, "q": q, "k": k, "v": v, **kv, "output": output, "lse": lse},
        {
            "g+": whole,
            "delta+": whole,
            "lse+": whole,
            "far_send+": (lines, 3 * heads + 1, far_rows, width),
        },
        scratch=((rows, width),),
        flops=block // GROUP,
    )
    column = exchange(mid.pop("far_send"), "seq", columns)
    own_rows = call(
        rows_kernel, offsets, mid, {"rows+": (heads + 1, quarter, width)}
    )["rows"]
    mid_rows = {
        f"rows{step}": turned(own_rows, step) if step else own_rows for step in range(GROUP)
    }
    term_shapes = {
        "scores": pairs,
        "terms": pairs,
        "keep": pairs,
        "mid_scores": mid_pairs,
        "mid_terms": mid_pairs,
        "mid_k": whole,
        "far_keep": (heads, far_rows, rows),
        "key_pairs": whole,
        "far_cols": (rows, heads * far_rows),
    }
    terms = call(
        terms_kernel,
        offsets,
        {
            "q": q, "k": k, "v": v, "g": mid["g"], "delta": mid["delta"], **kv,
            "drop_local": drop_local, "drop_mid": drop_mid, "drop_far": drop_far,
        },
        term_shapes,
        scratch=((rows, width), (rows, rows)),
        flops=2 * block,
    )
    column, own_rows, terms = lax.optimization_barrier((column, own_rows, terms))
    relay = call(
        relay_kernel,
        offsets,
        {"column": column, "q": q},
        {"relay+": (ACROSS, lines, 3 * heads + 1, far_rows, width)},
    )["relay"]
    far = exchange(relay, "seq", rows_of)
    stacked = call(
        grad_kernel,
        offsets,
        {
            "far": far, "q": q, "k": k, "g": mid["g"], "lse": mid["lse"],
            **{name: terms[name] for name in term_shapes}, **mid_rows, "kv0": kv["kv0"],
        },
        {"stacked+": (parts, 3, heads, rows // parts, width)},
        scratch=((rows, width),) * 2
        + (whole,)
        + ((rows, width),) * 6
        + (pairs, (count, 3 * heads + 1, far_rows, width)),
        flops=8 * block,
        fetched=("k", "rows1", "rows2", "rows3", *terms),
    )["stacked"]
    result = exchange(stacked, "head")
    shape = (parts * heads, rows // parts, width)
    return tuple(result[:, part].reshape(shape) for part in range(3))


def solution(mesh):
    tokens = P(None, ("seq", "head"), None)
    placed = P("head", "seq", None)
    return jax.shard_map(
        per_device,
        mesh=mesh,
        in_specs=(
            placed, placed, placed, placed, tokens,
            P("head", None), P("head"), placed, placed, P("head", None, None),
        ),
        out_specs=(tokens, tokens, tokens),
        check_vma=False,
    )
```

```python
import math

import jax
import jax.numpy as jnp
from jax import lax
from jax.experimental import pallas as pl
from jax.experimental.pallas import tpu as pltpu
from jax.sharding import PartitionSpec as P

GROUP = 4
HALF = GROUP // 2
LANES = 128
ACROSS = 4
KEEP_LEVEL = 7
KEEP_SCALE = 8.0 / 7.0
HIGHEST = lax.Precision.HIGHEST
NEG = -1e30


def dot(a, b, dims):
    return lax.dot_general(
        a, b, (dims, ((), ())), precision=HIGHEST, preferred_element_type=jnp.float32
    )


def dot_nt(a, b):
    return dot(a, b, ((1,), (1,)))


def dot_nn(a, b):
    return dot(a, b, ((1,), (0,)))


def dot_tn(a, b):
    return dot(a, b, ((0,), (0,)))


def wide(rows, lanes):
    if lanes <= LANES:
        return rows[:, :lanes]
    return jnp.concatenate([rows] * (lanes // LANES), axis=1)


def row_max(x):
    return jnp.broadcast_to(jnp.max(x, axis=1, keepdims=True), (x.shape[0], LANES))


def row_sum(x):
    return jnp.broadcast_to(jnp.sum(x, axis=1, keepdims=True), (x.shape[0], LANES))


def log_add(a, b):
    return jnp.maximum(a, b) + jnp.log(1.0 + jnp.exp(-jnp.abs(a - b)))


def masked_lse(scores, allowed):
    masked = jnp.where(allowed, scores, NEG)
    top = row_max(masked)
    return top + jnp.log(row_sum(jnp.exp(masked - wide(top, scores.shape[1]))))


def iotas(rows, cols):
    shape = (rows, cols)
    return lax.broadcasted_iota(jnp.int32, shape, 0), lax.broadcasted_iota(jnp.int32, shape, 1)


def spread_matrix(words, first, cols):
    source, column = iotas(4 * words, cols)
    column = column + first
    chosen = (column % 4 == source // words) & (column // 4 == source % words)
    return jnp.where(chosen, 1.0, 0.0).astype(jnp.bfloat16)


def keep_flags(words, axis):
    kept = [
        jnp.where(((words >> (3 * level)) & 7) < KEEP_LEVEL, 1.0, 0.0) for level in range(4)
    ]
    return jnp.concatenate(kept, axis=axis).astype(jnp.bfloat16)


def spread_flags(flags, spread, axis):
    whole = lax.dot_general(
        flags, spread, (((axis,), (0,)), ((), ())), preferred_element_type=jnp.float32
    )
    return whole * jnp.float32(KEEP_SCALE)


def pair_terms(scores, allowed, lse, delta, keep, grad_rows, values):
    cols = scores.shape[1]
    probs = jnp.where(allowed, jnp.exp(scores - wide(lse, cols)), 0.0)
    grad_probs = dot_nt(grad_rows, values) * keep
    return probs * keep, probs * (grad_probs - wide(delta, cols))


def place_info():
    place = lax.axis_index("seq")
    shifted = place + HALF
    return place, shifted // GROUP, shifted % GROUP


def place_masks(place, pos, quarter, rows):
    row, col = iotas(quarter, rows)
    return (col <= pos * quarter + row) & (place - pos + col // quarter >= 0)


def prep_kernel(mid_off, x, o):
    _, segment, pos = place_info()
    heads, rows, _ = x.k.shape
    words = x.drop_mid.shape[2]
    for head in range(heads):
        picked = pl.ds(mid_off[head, segment], rows // GROUP, stride=GROUP)
        mid_q, mid_k, mid_v = x.q[head, picked, :], x.k[head, picked, :], x.v[head, picked, :]
        mid_words = x.drop_mid[head].astype(jnp.float32)
        mid_words = jnp.concatenate([mid_words] * (LANES // words), axis=1)
        o.kv0[0, head] = mid_k
        o.kv0[1, head] = mid_v
        for step, ref in ((1, o.send1), (2, o.send2), (3, o.send3)):
            later = pos + step < GROUP
            ref[0, head] = jnp.where(later, mid_k, mid_q)
            ref[1, head] = jnp.where(later, mid_v, mid_words)


def local_kernel(mid_off, far_off, x, o):
    heads, rows, width = x.q.shape
    row, col = iotas(rows, rows)
    for head in range(heads):
        o.lse[head] = masked_lse(dot_nt(x.q[head], x.k[head]) * (width**-0.5), row >= col)


def gather_mid(x, side, head, buf):
    _, _, pos = place_info()
    quarter = x.kv0.shape[2]
    for distance in range(GROUP):
        start = ((pos - distance) % GROUP) * quarter
        buf[pl.ds(start, quarter), :] = x[f"kv{distance}"][side, head]


def mid_kernel(mid_off, far_off, x, o, buf):
    place, segment, pos = place_info()
    heads, rows, width = x.q.shape
    quarter = rows // GROUP
    count, sends = lax.axis_size("seq"), o.far_send.shape[0]
    far_rows = rows // count
    line = place // (count // sends)
    for head in range(heads):
        o.g[head] = x.g_parts[:, head].reshape(rows, width)
        far = pl.ds(far_off[head], far_rows, stride=count)
        far_q, far_k, far_v = x.q[head, far, :], x.k[head, far, :], x.v[head, far, :]
        far_g = o.g[head, far, :]
        for dest in range(sends):
            o.far_send[dest, head] = far_k
            o.far_send[dest, heads + head] = jnp.where(dest >= line, far_v, far_q)
            o.far_send[dest, 2 * heads + head] = far_g
    allowed = place_masks(place, pos, quarter, rows)
    _, lane = iotas(far_rows, LANES)
    part = lane // (LANES // (2 * heads))
    row_facts = jnp.zeros((far_rows, LANES), jnp.float32)
    for head in range(heads):
        o.delta[head] = row_sum(o.g[head] * x.output[head])
        gather_mid(x, 0, head, buf)
        mid = pl.ds(mid_off[head, segment], quarter, stride=GROUP)
        far = pl.ds(far_off[head], far_rows, stride=count)
        scores = dot_nt(x.q[head, mid, :], buf[...]) * (width**-0.5)
        o.lse[head] = x.lse[head]
        o.lse[head, mid, :] = log_add(x.lse[head, mid, :], masked_lse(scores, allowed))
        row_facts = jnp.where(part == 2 * head, o.lse[head, far, :], row_facts)
        row_facts = jnp.where(part == 2 * head + 1, o.delta[head, far, :], row_facts)
    for dest in range(sends):
        o.far_send[dest, 3 * heads] = row_facts


def relay_kernel(mid_off, far_off, x, o):
    place, _, _ = place_info()
    heads, rows, _ = x.q.shape
    sends = o.relay.shape[0]
    lines = x.column.shape[0]
    for dest in range(sends):
        o.relay[dest] = x.column[...]
    for head in range(heads):
        far_q = x.q[head, pl.ds(far_off[head], rows // (lines * sends), stride=lines * sends), :]
        far_v = x.column[place // sends, heads + head]
        for dest in range(sends):
            o.relay[dest, place // sends, heads + head] = jnp.where(
                dest >= place % sends, far_v, far_q
            )


def rows_kernel(mid_off, far_off, x, o):
    _, segment, _ = place_info()
    heads, rows, width = x.g.shape
    quarter = rows // GROUP
    _, lane = iotas(quarter, LANES)
    part = lane // (LANES // (2 * heads))
    facts = jnp.zeros((quarter, LANES), jnp.float32)
    for head in range(heads):
        mid = pl.ds(mid_off[head, segment], quarter, stride=GROUP)
        o.rows[head] = x.g[head, mid, :]
        facts = jnp.where(part == 2 * head, x.lse[head, mid, :], facts)
        facts = jnp.where(part == 2 * head + 1, x.delta[head, mid, :], facts)
    o.rows[heads] = facts


def terms_kernel(mid_off, far_off, x, o, buf, keep_buf):
    place, segment, pos = place_info()
    heads, rows, width = x.q.shape
    quarter = rows // GROUP
    scale = width**-0.5
    words = x.drop_local.shape[1]
    far_rows = o.far_keep.shape[1]
    key_spread = spread_matrix(words, pos * quarter, quarter)
    spread = spread_matrix(words, 0, rows)
    far_spread = spread_matrix(words, place * far_rows, far_rows)
    for head in range(heads):
        o.scores[head] = dot_nt(x.q[head], x.k[head]) * scale
        keep = spread_flags(keep_flags(x.drop_local[head], 0), spread, 0)
        o.keep[head] = keep
        o.terms[head] = dot_nt(x.g[head], x.v[head]) * keep - wide(x.delta[head], rows)
        mid = pl.ds(mid_off[head, segment], rows // GROUP, stride=GROUP)
        gather_mid(x, 0, head, buf)
        mid_q = x.q[head, mid, :]
        o.mid_k[head] = buf[...]
        o.mid_scores[head] = dot_nt(mid_q, buf[...]) * scale
        own_block = pl.ds(pos * quarter, quarter)
        buf[own_block, :] = mid_q
        o.key_pairs[head, :, 0:quarter] = dot_nt(buf[...], x.kv0[0, head]) * scale
        gather_mid(x, 1, head, buf)
        keep_buf[:, 0:words] = buf[:, 0:words]
        keep_buf[own_block, 0:words] = x.drop_mid[head].astype(jnp.float32)
        flags = keep_flags(keep_buf[:, 0:words].astype(jnp.int32), 1)
        o.key_pairs[head, :, quarter : 2 * quarter] = spread_flags(flags, key_spread, 1)
        keep = spread_flags(keep_flags(x.drop_mid[head], 1), spread, 1)
        o.mid_terms[head] = dot_nt(x.g[head, mid, :], buf[...]) * keep - wide(
            x.delta[head, mid, :], rows
        )
        flags = keep_flags(x.drop_far[head], 0)
        keep_buf[...] = spread_flags(flags, spread, 0)
        o.far_keep[head] = keep_buf[pl.ds(place * far_rows, far_rows), :]
        o.far_cols[:, head * far_rows : (head + 1) * far_rows] = spread_flags(flags, far_spread, 0)


def fact(facts, index, share):
    return jnp.broadcast_to(facts[:, index * share : index * share + 1], facts.shape)


def grad_kernel(
    mid_off, far_off, x, o, q_buf, lse_buf, far_lses, key_lse, gq_buf, gk_buf, gv_buf, mid_g,
    key_delta, score_buf, far_ref,
):
    place, segment, pos = place_info()
    heads, rows, width = x.q.shape
    quarter = rows // GROUP
    parts = o.stacked.shape[0]
    count = far_ref.shape[0]
    across, lines = x.far.shape[:2]
    for source in range(count):
        far_ref[source] = x.far[source % across, source // across]
    far_rows = rows // count
    scale = width**-0.5
    share = LANES // (2 * heads)
    row, col = iotas(rows, rows)
    causal = row >= col
    far_row, far_col = iotas(far_rows, rows)
    far_allowed = far_col <= place * far_rows + far_row
    key_row, key_col = iotas(rows, far_rows)
    far_key_allowed = place * far_rows + key_col <= key_row
    mid_allowed = place_masks(place, pos, quarter, rows)
    mid_row, mid_col = iotas(rows, quarter)
    block = mid_row // quarter
    mid_key_allowed = ((block > pos) & (place - pos + block < count)) | (
        (block == pos) & (mid_row % quarter >= mid_col)
    )
    own_block = pl.ds(pos * quarter, quarter)
    facts = far_ref[:, 3 * heads].reshape(rows, LANES)
    own = pl.ds(place * far_rows, far_rows)
    for head in range(heads):
        far = pl.ds(far_off[head], far_rows, stride=count)
        q_buf[...] = far_ref[:, heads + head].reshape(rows, width)
        q_buf[own, :] = x.q[head, far, :]
        all_k = far_ref[:, head].reshape(rows, width)
        score_buf[head] = dot_nt(q_buf[...], all_k) * scale
        far_lses[head] = log_add(
            fact(facts, 2 * head, share), masked_lse(score_buf[head], causal)
        )
    for head in range(heads):
        mid_start = mid_off[head, segment]
        mid = pl.ds(mid_start, quarter, stride=GROUP)
        far = pl.ds(far_off[head], far_rows, stride=count)
        all_k = far_ref[:, head].reshape(rows, width)
        all_v = far_ref[:, heads + head].reshape(rows, width)
        all_g = far_ref[:, 2 * heads + head].reshape(rows, width)
        q_buf[...] = all_v
        q_buf[own, :] = x.q[head, far, :]
        all_q = q_buf[...]
        far_lse = far_lses.at[head]
        lse_buf[...] = x.lse[head]
        lse_buf[far, :] = far_lse[own, :]

        probs = jnp.where(causal, jnp.exp(x.scores[head] - wide(lse_buf[...], rows)), 0.0)
        grad_scores = probs * x.terms[head]
        gq_buf[...] = dot_nn(grad_scores, x.k[head]) * scale
        gk_buf[...] = dot_tn(grad_scores, x.q[head]) * scale
        gv_buf[...] = dot_tn(probs * x.keep[head], x.g[head])

        probs = jnp.where(
            mid_allowed, jnp.exp(x.mid_scores[head] - wide(lse_buf[mid, :], rows)), 0.0
        )
        grad_scores = probs * x.mid_terms[head]
        gq_buf[mid, :] = gq_buf[mid, :] + dot_nn(grad_scores, x.mid_k[head]) * scale

        dropped, grad_scores = pair_terms(
            score_buf[head, own, :], far_allowed, lse_buf[far, :],
            fact(far_ref[place, 3 * heads], 2 * head + 1, share),
            x.far_keep[head], far_ref[place, 2 * heads + head], all_v,
        )
        gq_buf[far, :] = gq_buf[far, :] + dot_nn(grad_scores, all_k) * scale
        o.stacked[:, 0, head] = gq_buf[...].reshape(parts, rows // parts, width)

        meets = far_off[head] % GROUP == mid_start
        first = jnp.where(meets, (far_off[head] - mid_start) // GROUP, 0)
        for step in range(GROUP):
            source = (pos + step) % GROUP
            part = pl.ds(source * quarter, quarter)
            rows_ref = x[f"rows{(GROUP - step) % GROUP}"]
            mid_g[part, :] = rows_ref[head]
            key_delta[part, :] = fact(rows_ref[heads], 2 * head + 1, share)
            if step == 0:
                key_lse[part, :] = lse_buf[mid, :]
                continue
            key_lse[part, :] = fact(rows_ref[heads], 2 * head, share)
            spots = pl.ds(source * quarter + first, far_rows, stride=count // GROUP)
            start = jnp.clip(place - pos + source, 0, count - 1) * far_rows
            key_lse[spots, :] = jnp.where(
                meets, far_lse[pl.ds(start, far_rows), :], key_lse[spots, :]
            )
        q_buf[...] = x.mid_k[head]
        q_buf[own_block, :] = x.q[head, mid, :]
        probs = jnp.where(
            mid_key_allowed, jnp.exp(x.key_pairs[head, :, 0:quarter] - key_lse[:, 0:quarter]), 0.0
        )
        keep = x.key_pairs[head, :, quarter : 2 * quarter]
        grad_scores = probs * (
            dot_nt(mid_g[...], x.kv0[1, head]) * keep - key_delta[:, 0:quarter]
        )
        gk_buf[mid, :] = gk_buf[mid, :] + dot_tn(grad_scores, q_buf[...]) * scale
        gv_buf[mid, :] = gv_buf[mid, :] + dot_tn(probs * keep, mid_g[...])

        far_k, far_v = far_ref[place, head], far_ref[place, heads + head]
        dropped, grad_scores = pair_terms(
            dot_nt(all_q, far_k) * scale, far_key_allowed, far_lse[...],
            fact(facts, 2 * head + 1, share),
            x.far_cols[:, head * far_rows : (head + 1) * far_rows], all_g, far_v,
        )
        gk_buf[far, :] = gk_buf[far, :] + dot_tn(grad_scores, all_q) * scale
        gv_buf[far, :] = gv_buf[far, :] + dot_tn(dropped, all_g)
        o.stacked[:, 1, head] = gk_buf[...].reshape(parts, rows // parts, width)
        o.stacked[:, 2, head] = gv_buf[...].reshape(parts, rows // parts, width)


class Fetched:
    def __init__(self, ref, arrive):
        self.ref, self.shape, self.arrive = ref, ref.shape, arrive

    def __getitem__(self, index):
        self.arrive()
        return self.ref[index]


class Loaded:
    def __init__(self, refs):
        self.__dict__.update(refs=refs)

    def __getitem__(self, name):
        return self.refs[name]

    def __getattr__(self, name):
        return self.refs[name]


class Stored:
    def __init__(self, refs, sends):
        self.__dict__.update(refs, sends=sends)

    def send(self, name, part=slice(None)):
        self.sends(name, part)


def call(kernel, scalars, arrays, outs, scratch=(), flops=0, fetched=()):
    names = list(arrays)
    loads = [name for name in names if name in fetched]
    out_names = [name.rstrip("+") for name in outs]
    shapes = dict(zip(out_names, outs.values()))
    saves = [name for name in outs if not name.endswith("+")]
    hbm, vmem = pl.BlockSpec(memory_space=pltpu.HBM), pl.BlockSpec(memory_space=pltpu.VMEM)

    def run(*refs):
        refs = list(refs)

        def take(count):
            taken, refs[:] = refs[:count], refs[count:]
            return taken

        scalar_refs, in_refs, out_refs = take(len(scalars)), take(len(names)), take(len(outs))
        in_bufs, out_bufs, extra = take(len(loads)), take(len(saves)), take(len(scratch))
        in_sems, out_sems = refs
        given, written = dict(zip(names, in_refs)), dict(zip(out_names, out_refs))
        copies = [
            pltpu.make_async_copy(given[name], buf, in_sems.at[i])
            for i, (name, buf) in enumerate(zip(loads, in_bufs))
        ]
        for copy in copies:
            copy.start()

        def arrive():
            while copies:
                copies.pop(0).wait()

        loaded = Loaded(
            {**given, **{name: Fetched(buf, arrive) for name, buf in zip(loads, in_bufs)}}
        )
        buffers = dict(zip(saves, out_bufs))
        writes = []

        def send(name, part=slice(None)):
            write = pltpu.make_async_copy(
                buffers[name].at[part], written[name].at[part], out_sems.at[len(writes)]
            )
            write.start()
            writes.append(write)
            sent.add(name)

        sent = set()
        kernel(*scalar_refs, loaded, Stored({**written, **buffers}, send), *extra)
        arrive()
        for name in saves:
            if name not in sent:
                send(name)
        for write in writes:
            write.wait()

    values = list(arrays.values())
    moved = 4 * sum(math.prod(shape) for shape in [v.shape for v in values] + [*shapes.values()])
    result = pl.pallas_call(
        run,
        out_shape=[
            pltpu.HBM(shape, jnp.float32)
            if name in saves
            else jax.ShapeDtypeStruct(shape, jnp.float32)
            for name, shape in shapes.items()
        ],
        in_specs=[pl.BlockSpec(memory_space=pltpu.SMEM)] * len(scalars)
        + [hbm if name in loads else vmem for name in names],
        out_specs=[hbm if name in saves else vmem for name in shapes],
        scratch_shapes=[pltpu.VMEM(arrays[name].shape, arrays[name].dtype) for name in loads]
        + [pltpu.VMEM(shapes[name], jnp.float32) for name in saves]
        + [pltpu.VMEM(shape, jnp.float32) for shape in scratch]
        + [
            pltpu.SemaphoreType.DMA((max(len(loads), 1),)),
            pltpu.SemaphoreType.DMA((max(2 * len(saves), 1),)),
        ],
        cost_estimate=pl.CostEstimate(flops=flops, transcendentals=0, bytes_accessed=moved),
        compiler_params=pltpu.CompilerParams(vmem_limit_bytes=40 * 1024 * 1024),
    )(
        *scalars,
        *[
            pltpu.with_memory_space_constraint(value, pltpu.HBM) if name in loads else value
            for name, value in arrays.items()
        ],
    )
    return dict(zip(out_names, result))


def turned(value, steps, back_only=False):
    count = lax.axis_size("seq")
    pairs = []
    for first in range(-HALF, count - HALF, GROUP):
        for pos in range(GROUP):
            source, target = first + pos, first + (pos + steps) % GROUP
            crosses = (source < count) != (target < count) or (source < 0) != (target < 0)
            if crosses or (back_only and target > source):
                continue
            pairs.append((source % count, target % count))
    return lax.ppermute(value, "seq", pairs)


def exchange(value, axis, groups=None):
    return lax.all_to_all(
        value, axis, split_axis=0, concat_axis=0, tiled=True, axis_index_groups=groups
    )


def per_device(q, k, v, output, grad_output, mid_off, far_off, drop_local, drop_mid, drop_far):
    heads, rows, width = q.shape
    count = lax.axis_size("seq")
    parts = lax.axis_size("head")
    quarter = rows // GROUP
    far_rows = rows // count
    whole = (heads, rows, width)
    pairs = (heads, rows, rows)
    mid_pairs = (heads, quarter, rows)
    key_pairs = (heads, rows, quarter)
    block = 6 * 2 * heads * rows * rows * width
    drop_local = jnp.swapaxes(drop_local, 1, 2)
    drop_far = jnp.swapaxes(drop_far, 1, 2)
    offsets = (mid_off, far_off)
    lines = count // ACROSS
    rows_of = [[line * ACROSS + i for i in range(ACROSS)] for line in range(lines)]
    columns = [list(group) for group in zip(*rows_of)]

    g_parts = exchange(grad_output.reshape(parts, heads, rows // parts, width), "head")
    first = call(
        prep_kernel,
        (mid_off,),
        {"q": q, "k": k, "v": v, "drop_mid": drop_mid},
        {f"{name}+": (2, heads, quarter, width) for name in ("kv0", "send1", "send2", "send3")},
        fetched=("v", "drop_mid"),
    )
    kv = {
        f"kv{step}": turned(first[f"send{step}"], step) if step else first["kv0"]
        for step in range(GROUP)
    }
    lse = call(local_kernel, offsets, {"q": q, "k": k}, {"lse+": whole}, flops=block)["lse"]
    mid = call(
        mid_kernel,
        offsets,
        {"g_parts": g_parts, "q": q, "k": k, "v": v, **kv, "output": output, "lse": lse},
        {
            "g+": whole,
            "delta+": whole,
            "lse+": whole,
            "far_send+": (lines, 3 * heads + 1, far_rows, width),
        },
        scratch=((rows, width),),
        flops=block // GROUP,
    )
    column = exchange(mid.pop("far_send"), "seq", columns)
    own_rows = call(
        rows_kernel, offsets, mid, {"rows+": (heads + 1, quarter, width)}
    )["rows"]
    mid_rows = {
        f"rows{step}": turned(own_rows, step, True) if step else own_rows for step in range(GROUP)
    }
    term_shapes = {
        "scores": pairs,
        "terms": pairs,
        "keep": pairs,
        "mid_scores": mid_pairs,
        "mid_terms": mid_pairs,
        "mid_k": whole,
        "far_keep": (heads, far_rows, rows),
        "key_pairs": whole,
        "far_cols": (rows, heads * far_rows),
    }
    terms = call(
        terms_kernel,
        offsets,
        {
            "q": q, "k": k, "v": v, "g": mid["g"], "delta": mid["delta"], **kv,
            "drop_local": drop_local, "drop_mid": drop_mid, "drop_far": drop_far,
        },
        term_shapes,
        scratch=((rows, width), (rows, rows)),
        flops=2 * block,
    )
    column, own_rows, terms = lax.optimization_barrier((column, own_rows, terms))
    relay = call(
        relay_kernel,
        offsets,
        {"column": column, "q": q},
        {"relay+": (ACROSS, lines, 3 * heads + 1, far_rows, width)},
    )["relay"]
    far = exchange(relay, "seq", rows_of)
    stacked = call(
        grad_kernel,
        offsets,
        {
            "far": far, "q": q, "k": k, "g": mid["g"], "lse": mid["lse"],
            **{name: terms[name] for name in term_shapes}, **mid_rows, "kv0": kv["kv0"],
        },
        {"stacked+": (parts, 3, heads, rows // parts, width)},
        scratch=((rows, width),) * 2
        + (whole,)
        + ((rows, width),) * 6
        + (pairs, (count, 3 * heads + 1, far_rows, width)),
        flops=8 * block,
        fetched=("k", "rows1", "rows2", "rows3", *terms),
    )["stacked"]
    result = exchange(stacked, "head")
    shape = (parts * heads, rows // parts, width)
    return tuple(result[:, part].reshape(shape) for part in range(3))


def solution(mesh):
    tokens = P(None, ("seq", "head"), None)
    placed = P("head", "seq", None)
    return jax.shard_map(
        per_device,
        mesh=mesh,
        in_specs=(
            placed, placed, placed, placed, tokens,
            P("head", None), P("head"), placed, placed, P("head", None, None),
        ),
        out_specs=(tokens, tokens, tokens),
        check_vma=False,
    )
```

```python
import math

import jax
import jax.numpy as jnp
from jax import lax
from jax.experimental import pallas as pl
from jax.experimental.pallas import tpu as pltpu
from jax.sharding import PartitionSpec as P

GROUP = 4
HALF = GROUP // 2
LANES = 128
ACROSS = 4
KEEP_LEVEL = 7
KEEP_SCALE = 8.0 / 7.0
HIGHEST = lax.Precision.HIGHEST
NEG = -1e30


def dot(a, b, dims):
    return lax.dot_general(
        a, b, (dims, ((), ())), precision=HIGHEST, preferred_element_type=jnp.float32
    )


def dot_nt(a, b):
    return dot(a, b, ((1,), (1,)))


def dot_nn(a, b):
    return dot(a, b, ((1,), (0,)))


def dot_tn(a, b):
    return dot(a, b, ((0,), (0,)))


def wide(rows, lanes):
    if lanes <= LANES:
        return rows[:, :lanes]
    return jnp.concatenate([rows] * (lanes // LANES), axis=1)


def row_max(x):
    return jnp.broadcast_to(jnp.max(x, axis=1, keepdims=True), (x.shape[0], LANES))


def row_sum(x):
    return jnp.broadcast_to(jnp.sum(x, axis=1, keepdims=True), (x.shape[0], LANES))


def log_add(a, b):
    return jnp.maximum(a, b) + jnp.log(1.0 + jnp.exp(-jnp.abs(a - b)))


def masked_lse(scores, allowed):
    masked = jnp.where(allowed, scores, NEG)
    top = row_max(masked)
    return top + jnp.log(row_sum(jnp.exp(masked - wide(top, scores.shape[1]))))


def iotas(rows, cols):
    shape = (rows, cols)
    return lax.broadcasted_iota(jnp.int32, shape, 0), lax.broadcasted_iota(jnp.int32, shape, 1)


def spread_matrix(words, first, cols):
    source, column = iotas(4 * words, cols)
    column = column + first
    chosen = (column % 4 == source // words) & (column // 4 == source % words)
    return jnp.where(chosen, 1.0, 0.0).astype(jnp.bfloat16)


def keep_flags(words, axis):
    kept = [
        jnp.where(((words >> (3 * level)) & 7) < KEEP_LEVEL, 1.0, 0.0) for level in range(4)
    ]
    return jnp.concatenate(kept, axis=axis).astype(jnp.bfloat16)


def spread_flags(flags, spread, axis):
    whole = lax.dot_general(
        flags, spread, (((axis,), (0,)), ((), ())), preferred_element_type=jnp.float32
    )
    return whole * jnp.float32(KEEP_SCALE)


def pair_terms(scores, allowed, lse, delta, keep, grad_rows, values):
    cols = scores.shape[1]
    probs = jnp.where(allowed, jnp.exp(scores - wide(lse, cols)), 0.0)
    grad_probs = dot_nt(grad_rows, values) * keep
    return probs * keep, probs * (grad_probs - wide(delta, cols))


def place_info():
    place = lax.axis_index("seq")
    shifted = place + HALF
    return place, shifted // GROUP, shifted % GROUP


def place_masks(place, pos, quarter, rows):
    row, col = iotas(quarter, rows)
    return (col <= pos * quarter + row) & (place - pos + col // quarter >= 0)


def prep_kernel(mid_off, x, o):
    _, segment, pos = place_info()
    heads, rows, _ = x.k.shape
    words = x.drop_mid.shape[2]
    for head in range(heads):
        picked = pl.ds(mid_off[head, segment], rows // GROUP, stride=GROUP)
        mid_q, mid_k, mid_v = x.q[head, picked, :], x.k[head, picked, :], x.v[head, picked, :]
        mid_words = x.drop_mid[head].astype(jnp.float32)
        mid_words = jnp.concatenate([mid_words] * (LANES // words), axis=1)
        o.kv0[0, head] = mid_k
        o.kv0[1, head] = mid_v
        for step, ref in ((1, o.send1), (2, o.send2), (3, o.send3)):
            later = pos + step < GROUP
            ref[0, head] = jnp.where(later, mid_k, mid_q)
            ref[1, head] = jnp.where(later, mid_v, mid_words)


def local_kernel(mid_off, far_off, x, o):
    heads, rows, width = x.q.shape
    row, col = iotas(rows, rows)
    for head in range(heads):
        o.lse[head] = masked_lse(dot_nt(x.q[head], x.k[head]) * (width**-0.5), row >= col)


def gather_mid(x, side, head, buf):
    _, _, pos = place_info()
    quarter = x.kv0.shape[2]
    for distance in range(GROUP):
        start = ((pos - distance) % GROUP) * quarter
        buf[pl.ds(start, quarter), :] = x[f"kv{distance}"][side, head]


def mid_kernel(mid_off, far_off, x, o, buf):
    place, segment, pos = place_info()
    heads, rows, width = x.q.shape
    quarter = rows // GROUP
    count, sends = lax.axis_size("seq"), o.far_send.shape[0]
    far_rows = rows // count
    line = place // (count // sends)
    for head in range(heads):
        o.g[head] = x.g_parts[:, head].reshape(rows, width)
        far = pl.ds(far_off[head], far_rows, stride=count)
        far_q, far_k, far_v = x.q[head, far, :], x.k[head, far, :], x.v[head, far, :]
        far_g = o.g[head, far, :]
        for dest in range(sends):
            o.far_send[dest, head] = far_k
            o.far_send[dest, heads + head] = jnp.where(dest >= line, far_v, far_q)
            o.far_send[dest, 2 * heads + head] = far_g
    allowed = place_masks(place, pos, quarter, rows)
    _, lane = iotas(far_rows, LANES)
    part = lane // (LANES // (2 * heads))
    row_facts = jnp.zeros((far_rows, LANES), jnp.float32)
    for head in range(heads):
        o.delta[head] = row_sum(o.g[head] * x.output[head])
        gather_mid(x, 0, head, buf)
        mid = pl.ds(mid_off[head, segment], quarter, stride=GROUP)
        far = pl.ds(far_off[head], far_rows, stride=count)
        scores = dot_nt(x.q[head, mid, :], buf[...]) * (width**-0.5)
        o.lse[head] = x.lse[head]
        o.lse[head, mid, :] = log_add(x.lse[head, mid, :], masked_lse(scores, allowed))
        row_facts = jnp.where(part == 2 * head, o.lse[head, far, :], row_facts)
        row_facts = jnp.where(part == 2 * head + 1, o.delta[head, far, :], row_facts)
    for dest in range(sends):
        o.far_send[dest, 3 * heads] = row_facts


def relay_kernel(mid_off, far_off, x, o):
    place, _, _ = place_info()
    heads, rows, _ = x.q.shape
    sends = o.relay.shape[0]
    lines = x.column.shape[0]
    for dest in range(sends):
        o.relay[dest] = x.column[...]
    for head in range(heads):
        far_q = x.q[head, pl.ds(far_off[head], rows // (lines * sends), stride=lines * sends), :]
        far_v = x.column[place // sends, heads + head]
        for dest in range(sends):
            o.relay[dest, place // sends, heads + head] = jnp.where(
                dest >= place % sends, far_v, far_q
            )


def rows_kernel(mid_off, far_off, x, o):
    _, segment, _ = place_info()
    heads, rows, width = x.g.shape
    quarter = rows // GROUP
    _, lane = iotas(quarter, LANES)
    part = lane // (LANES // (2 * heads))
    facts = jnp.zeros((quarter, LANES), jnp.float32)
    for head in range(heads):
        mid = pl.ds(mid_off[head, segment], quarter, stride=GROUP)
        o.rows[head] = x.g[head, mid, :]
        facts = jnp.where(part == 2 * head, x.lse[head, mid, :], facts)
        facts = jnp.where(part == 2 * head + 1, x.delta[head, mid, :], facts)
    o.rows[heads] = facts


def terms_kernel(mid_off, far_off, x, o, buf, keep_buf):
    place, segment, pos = place_info()
    heads, rows, width = x.q.shape
    quarter = rows // GROUP
    scale = width**-0.5
    words = x.drop_local.shape[1]
    far_rows = o.far_keep.shape[1]
    key_spread = spread_matrix(words, pos * quarter, quarter)
    spread = spread_matrix(words, 0, rows)
    far_spread = spread_matrix(words, place * far_rows, far_rows)
    for head in range(heads):
        o.scores[head] = dot_nt(x.q[head], x.k[head]) * scale
        keep = spread_flags(keep_flags(x.drop_local[head], 0), spread, 0)
        o.keep[head] = keep
        o.terms[head] = dot_nt(x.g[head], x.v[head]) * keep - wide(x.delta[head], rows)
        mid = pl.ds(mid_off[head, segment], rows // GROUP, stride=GROUP)
        gather_mid(x, 0, head, buf)
        mid_q = x.q[head, mid, :]
        o.mid_k[head] = buf[...]
        o.mid_scores[head] = dot_nt(mid_q, buf[...]) * scale
        own_block = pl.ds(pos * quarter, quarter)
        buf[own_block, :] = mid_q
        o.key_pairs[head, :, 0:quarter] = dot_nt(buf[...], x.kv0[0, head]) * scale
        gather_mid(x, 1, head, buf)
        keep_buf[:, 0:words] = buf[:, 0:words]
        keep_buf[own_block, 0:words] = x.drop_mid[head].astype(jnp.float32)
        flags = keep_flags(keep_buf[:, 0:words].astype(jnp.int32), 1)
        o.key_pairs[head, :, quarter : 2 * quarter] = spread_flags(flags, key_spread, 1)
        keep = spread_flags(keep_flags(x.drop_mid[head], 1), spread, 1)
        o.mid_terms[head] = dot_nt(x.g[head, mid, :], buf[...]) * keep - wide(
            x.delta[head, mid, :], rows
        )
        flags = keep_flags(x.drop_far[head], 0)
        keep_buf[...] = spread_flags(flags, spread, 0)
        o.far_keep[head] = keep_buf[pl.ds(place * far_rows, far_rows), :]
        o.far_cols[:, head * far_rows : (head + 1) * far_rows] = spread_flags(flags, far_spread, 0)


def fact(facts, index, share):
    return jnp.broadcast_to(facts[:, index * share : index * share + 1], facts.shape)


def grad_kernel(
    mid_off, far_off, x, o, q_buf, lse_buf, far_lses, key_lse, gq_buf, gk_buf, gv_buf, mid_g,
    key_delta, score_buf, far_ref,
):
    place, segment, pos = place_info()
    heads, rows, width = x.q.shape
    quarter = rows // GROUP
    parts = o.stacked.shape[0]
    count = far_ref.shape[0]
    across, lines = x.far.shape[:2]
    for source in range(count):
        far_ref[source] = x.far[source % across, source // across]
    far_rows = rows // count
    scale = width**-0.5
    share = LANES // (2 * heads)
    row, col = iotas(rows, rows)
    causal = row >= col
    far_row, far_col = iotas(far_rows, rows)
    far_allowed = far_col <= place * far_rows + far_row
    key_row, key_col = iotas(rows, far_rows)
    far_key_allowed = place * far_rows + key_col <= key_row
    mid_allowed = place_masks(place, pos, quarter, rows)
    mid_row, mid_col = iotas(rows, quarter)
    block = mid_row // quarter
    mid_key_allowed = ((block > pos) & (place - pos + block < count)) | (
        (block == pos) & (mid_row % quarter >= mid_col)
    )
    own_block = pl.ds(pos * quarter, quarter)
    facts = far_ref[:, 3 * heads].reshape(rows, LANES)
    own = pl.ds(place * far_rows, far_rows)
    for head in range(heads):
        far = pl.ds(far_off[head], far_rows, stride=count)
        q_buf[...] = far_ref[:, heads + head].reshape(rows, width)
        q_buf[own, :] = x.q[head, far, :]
        all_k = far_ref[:, head].reshape(rows, width)
        score_buf[head] = dot_nt(q_buf[...], all_k) * scale
        far_lses[head] = log_add(
            fact(facts, 2 * head, share), masked_lse(score_buf[head], causal)
        )
    for head in range(heads):
        mid_start = mid_off[head, segment]
        mid = pl.ds(mid_start, quarter, stride=GROUP)
        far = pl.ds(far_off[head], far_rows, stride=count)
        all_k = far_ref[:, head].reshape(rows, width)
        all_v = far_ref[:, heads + head].reshape(rows, width)
        all_g = far_ref[:, 2 * heads + head].reshape(rows, width)
        q_buf[...] = all_v
        q_buf[own, :] = x.q[head, far, :]
        all_q = q_buf[...]
        far_lse = far_lses.at[head]
        lse_buf[...] = x.lse[head]
        lse_buf[far, :] = far_lse[own, :]

        probs = jnp.where(causal, jnp.exp(x.scores[head] - wide(lse_buf[...], rows)), 0.0)
        grad_scores = probs * x.terms[head]
        gq_buf[...] = dot_nn(grad_scores, x.k[head]) * scale
        gk_buf[...] = dot_tn(grad_scores, x.q[head]) * scale
        gv_buf[...] = dot_tn(probs * x.keep[head], x.g[head])

        probs = jnp.where(
            mid_allowed, jnp.exp(x.mid_scores[head] - wide(lse_buf[mid, :], rows)), 0.0
        )
        grad_scores = probs * x.mid_terms[head]
        gq_buf[mid, :] = gq_buf[mid, :] + dot_nn(grad_scores, x.mid_k[head]) * scale

        dropped, grad_scores = pair_terms(
            score_buf[head, own, :], far_allowed, lse_buf[far, :],
            fact(far_ref[place, 3 * heads], 2 * head + 1, share),
            x.far_keep[head], far_ref[place, 2 * heads + head], all_v,
        )
        gq_buf[far, :] = gq_buf[far, :] + dot_nn(grad_scores, all_k) * scale
        o.stacked[:, 0, head] = gq_buf[...].reshape(parts, rows // parts, width)

        meets = far_off[head] % GROUP == mid_start
        first = jnp.where(meets, (far_off[head] - mid_start) // GROUP, 0)
        for step in range(GROUP):
            source = (pos + step) % GROUP
            part = pl.ds(source * quarter, quarter)
            rows_ref = x[f"rows{(GROUP - step) % GROUP}"]
            mid_g[part, :] = rows_ref[head]
            key_delta[part, :] = fact(rows_ref[heads], 2 * head + 1, share)
            if step == 0:
                key_lse[part, :] = lse_buf[mid, :]
                continue
            key_lse[part, :] = fact(rows_ref[heads], 2 * head, share)
            spots = pl.ds(source * quarter + first, far_rows, stride=count // GROUP)
            start = jnp.clip(place - pos + source, 0, count - 1) * far_rows
            key_lse[spots, :] = jnp.where(
                meets, far_lse[pl.ds(start, far_rows), :], key_lse[spots, :]
            )
        q_buf[...] = x.mid_k[head]
        q_buf[own_block, :] = x.q[head, mid, :]
        probs = jnp.where(
            mid_key_allowed, jnp.exp(x.key_pairs[head, :, 0:quarter] - key_lse[:, 0:quarter]), 0.0
        )
        keep = x.key_pairs[head, :, quarter : 2 * quarter]
        grad_scores = probs * (
            dot_nt(mid_g[...], x.kv0[1, head]) * keep - key_delta[:, 0:quarter]
        )
        gk_buf[mid, :] = gk_buf[mid, :] + dot_tn(grad_scores, q_buf[...]) * scale
        gv_buf[mid, :] = gv_buf[mid, :] + dot_tn(probs * keep, mid_g[...])

        far_k, far_v = far_ref[place, head], far_ref[place, heads + head]
        dropped, grad_scores = pair_terms(
            dot_nt(all_q, far_k) * scale, far_key_allowed, far_lse[...],
            fact(facts, 2 * head + 1, share),
            x.far_cols[:, head * far_rows : (head + 1) * far_rows], all_g, far_v,
        )
        gk_buf[far, :] = gk_buf[far, :] + dot_tn(grad_scores, all_q) * scale
        gv_buf[far, :] = gv_buf[far, :] + dot_tn(dropped, all_g)
        o.stacked[:, 1, head] = gk_buf[...].reshape(parts, rows // parts, width)
        o.stacked[:, 2, head] = gv_buf[...].reshape(parts, rows // parts, width)


class Fetched:
    def __init__(self, ref, arrive):
        self.ref, self.shape, self.arrive = ref, ref.shape, arrive

    def __getitem__(self, index):
        self.arrive()
        return self.ref[index]


class Loaded:
    def __init__(self, refs):
        self.__dict__.update(refs=refs)

    def __getitem__(self, name):
        return self.refs[name]

    def __getattr__(self, name):
        return self.refs[name]


class Stored:
    def __init__(self, refs, sends):
        self.__dict__.update(refs, sends=sends)

    def send(self, name, part=slice(None)):
        self.sends(name, part)


def call(kernel, scalars, arrays, outs, scratch=(), flops=0, fetched=()):
    names = list(arrays)
    loads = [name for name in names if name in fetched]
    out_names = [name.rstrip("+") for name in outs]
    shapes = dict(zip(out_names, outs.values()))
    saves = [name for name in outs if not name.endswith("+")]
    hbm, vmem = pl.BlockSpec(memory_space=pltpu.HBM), pl.BlockSpec(memory_space=pltpu.VMEM)

    def run(*refs):
        refs = list(refs)

        def take(count):
            taken, refs[:] = refs[:count], refs[count:]
            return taken

        scalar_refs, in_refs, out_refs = take(len(scalars)), take(len(names)), take(len(outs))
        in_bufs, out_bufs, extra = take(len(loads)), take(len(saves)), take(len(scratch))
        in_sems, out_sems = refs
        given, written = dict(zip(names, in_refs)), dict(zip(out_names, out_refs))
        copies = [
            pltpu.make_async_copy(given[name], buf, in_sems.at[i])
            for i, (name, buf) in enumerate(zip(loads, in_bufs))
        ]
        for copy in copies:
            copy.start()

        def arrive():
            while copies:
                copies.pop(0).wait()

        loaded = Loaded(
            {**given, **{name: Fetched(buf, arrive) for name, buf in zip(loads, in_bufs)}}
        )
        buffers = dict(zip(saves, out_bufs))
        writes = []

        def send(name, part=slice(None)):
            write = pltpu.make_async_copy(
                buffers[name].at[part], written[name].at[part], out_sems.at[len(writes)]
            )
            write.start()
            writes.append(write)
            sent.add(name)

        sent = set()
        kernel(*scalar_refs, loaded, Stored({**written, **buffers}, send), *extra)
        arrive()
        for name in saves:
            if name not in sent:
                send(name)
        for write in writes:
            write.wait()

    values = list(arrays.values())
    moved = 4 * sum(math.prod(shape) for shape in [v.shape for v in values] + [*shapes.values()])
    result = pl.pallas_call(
        run,
        out_shape=[
            pltpu.HBM(shape, jnp.float32)
            if name in saves
            else jax.ShapeDtypeStruct(shape, jnp.float32)
            for name, shape in shapes.items()
        ],
        in_specs=[pl.BlockSpec(memory_space=pltpu.SMEM)] * len(scalars)
        + [hbm if name in loads else vmem for name in names],
        out_specs=[hbm if name in saves else vmem for name in shapes],
        scratch_shapes=[pltpu.VMEM(arrays[name].shape, arrays[name].dtype) for name in loads]
        + [pltpu.VMEM(shapes[name], jnp.float32) for name in saves]
        + [pltpu.VMEM(shape, jnp.float32) for shape in scratch]
        + [
            pltpu.SemaphoreType.DMA((max(len(loads), 1),)),
            pltpu.SemaphoreType.DMA((max(2 * len(saves), 1),)),
        ],
        cost_estimate=pl.CostEstimate(flops=flops, transcendentals=0, bytes_accessed=moved),
        compiler_params=pltpu.CompilerParams(vmem_limit_bytes=40 * 1024 * 1024),
    )(
        *scalars,
        *[
            pltpu.with_memory_space_constraint(value, pltpu.HBM) if name in loads else value
            for name, value in arrays.items()
        ],
    )
    return dict(zip(out_names, result))


def turned(value, steps, back_only=False):
    count = lax.axis_size("seq")
    pairs = []
    for first in range(-HALF, count - HALF, GROUP):
        for pos in range(GROUP):
            source, target = first + pos, first + (pos + steps) % GROUP
            crosses = (source < count) != (target < count) or (source < 0) != (target < 0)
            if crosses or (back_only and target > source):
                continue
            pairs.append((source % count, target % count))
    return lax.ppermute(value, "seq", pairs)


def exchange(value, axis, groups=None):
    return lax.all_to_all(
        value, axis, split_axis=0, concat_axis=0, tiled=True, axis_index_groups=groups
    )


def per_device(q, k, v, output, grad_output, mid_off, far_off, drop_local, drop_mid, drop_far):
    heads, rows, width = q.shape
    count = lax.axis_size("seq")
    parts = lax.axis_size("head")
    quarter = rows // GROUP
    far_rows = rows // count
    whole = (heads, rows, width)
    pairs = (heads, rows, rows)
    mid_pairs = (heads, quarter, rows)
    key_pairs = (heads, rows, quarter)
    block = 6 * 2 * heads * rows * rows * width
    drop_local = jnp.swapaxes(drop_local, 1, 2)
    drop_far = jnp.swapaxes(drop_far, 1, 2)
    offsets = (mid_off, far_off)
    lines = count // ACROSS
    rows_of = [[line * ACROSS + i for i in range(ACROSS)] for line in range(lines)]
    columns = [list(group) for group in zip(*rows_of)]

    g_parts = exchange(grad_output.reshape(parts, heads, rows // parts, width), "head")
    first = call(
        prep_kernel,
        (mid_off,),
        {"q": q, "k": k, "v": v, "drop_mid": drop_mid},
        {f"{name}+": (2, heads, quarter, width) for name in ("kv0", "send1", "send2", "send3")},
        fetched=("v", "drop_mid"),
    )
    kv = {
        f"kv{step}": turned(first[f"send{step}"], step) if step else first["kv0"]
        for step in range(GROUP)
    }
    lse = call(local_kernel, offsets, {"q": q, "k": k}, {"lse+": whole}, flops=block)["lse"]
    mid = call(
        mid_kernel,
        offsets,
        {"g_parts": g_parts, "q": q, "k": k, "v": v, **kv, "output": output, "lse": lse},
        {
            "g+": whole,
            "delta+": whole,
            "lse+": whole,
            "far_send+": (lines, 3 * heads + 1, far_rows, width),
        },
        scratch=((rows, width),),
        flops=block // GROUP,
    )
    column = exchange(mid.pop("far_send"), "seq", columns)
    own_rows = call(
        rows_kernel, offsets, mid, {"rows+": (heads + 1, quarter, width)}
    )["rows"]
    mid_rows = {
        f"rows{step}": turned(own_rows, step, True) if step else own_rows for step in range(GROUP)
    }
    term_shapes = {
        "scores": pairs,
        "terms": pairs,
        "keep": pairs,
        "mid_scores": mid_pairs,
        "mid_terms": mid_pairs,
        "mid_k": whole,
        "far_keep": (heads, far_rows, rows),
        "key_pairs": whole,
        "far_cols": (rows, heads * far_rows),
    }
    terms = call(
        terms_kernel,
        offsets,
        {
            "q": q, "k": k, "v": v, "g": mid["g"], "delta": mid["delta"], **kv,
            "drop_local": drop_local, "drop_mid": drop_mid, "drop_far": drop_far,
        },
        term_shapes,
        scratch=((rows, width), (rows, rows)),
        flops=2 * block,
    )
    column, mid_rows = lax.optimization_barrier((column, mid_rows))
    relay = call(
        relay_kernel,
        offsets,
        {"column": column, "q": q},
        {"relay+": (ACROSS, lines, 3 * heads + 1, far_rows, width)},
    )["relay"]
    far = exchange(relay, "seq", rows_of)
    stacked = call(
        grad_kernel,
        offsets,
        {
            "far": far, "q": q, "k": k, "g": mid["g"], "lse": mid["lse"],
            **{name: terms[name] for name in term_shapes}, **mid_rows, "kv0": kv["kv0"],
        },
        {"stacked+": (parts, 3, heads, rows // parts, width)},
        scratch=((rows, width),) * 2
        + (whole,)
        + ((rows, width),) * 6
        + (pairs, (count, 3 * heads + 1, far_rows, width)),
        flops=8 * block,
        fetched=("k", "rows1", "rows2", "rows3", *terms),
    )["stacked"]
    result = exchange(stacked, "head")
    shape = (parts * heads, rows // parts, width)
    return tuple(result[:, part].reshape(shape) for part in range(3))


def solution(mesh):
    tokens = P(None, ("seq", "head"), None)
    placed = P("head", "seq", None)
    return jax.shard_map(
        per_device,
        mesh=mesh,
        in_specs=(
            placed, placed, placed, placed, tokens,
            P("head", None), P("head"), placed, placed, P("head", None, None),
        ),
        out_specs=(tokens, tokens, tokens),
        check_vma=False,
    )
```
